256 devices in a mesh: session: 8 (over x_lo, y), ctx: 32 (over x_hi, z, core).
Axes of the slice: x: 4 (x_hi: 2, x_lo: 2; x = x_hi * 2 + x_lo), y: 4, z: 8, core: 2. Of those that a mesh axis runs over, the one named last changes fastest.
Arguments:
- frames: float32 [49152, 1024], P(('session', 'ctx')), parts along dimension 0, may hold values from -6 to 6
- attend_gain: float32 [1024], replicated, may hold values from 0.25 to 1.75
- query_weight: bfloat16 [1024, 1024], replicated, may hold values from -8 to 8
- key_weight: bfloat16 [1024, 1024], replicated, may hold values from -8 to 8
- value_weight: bfloat16 [1024, 1024], replicated, may hold values from -0.1875 to 0.1875
- output_weight: bfloat16 [1024, 1024], replicated, may hold values from -0.1875 to 0.1875
- mixer_gain: float32 [1024], replicated, may hold values from 0.25 to 1.75
- depthwise: float32 [31, 1024], replicated, may hold values from -1 to 1
- mixer_bias: float32 [1024], replicated, may hold values from -3 to 3
Outputs:
- block_out: float32 [49152, 1024], P(('session', 'ctx')), parts along dimension 0
The draws below stay inside these ranges and needn't reach their ends.
There are 8 independent parts, one for each index of `session`. The reference program is written for one: setup_inputs(seed, part) draws one part's arguments, and reference() takes and returns one part's arrays. A program takes and returns all parts, laid end to end along the dimension named above; an argument that names none is the same for every part. Nothing has to cross between parts.
All inputs are finite; a program needn't handle non-finite values.
Results may differ from the reference program's by a relative error of at most 0.0031.
Values may be sent and summed in bfloat16 or wider, within the bound.
A program may use at most 256 MiB of HBM per device.

```python
import jax
import jax.numpy as jnp
from jax import lax

D = 1024
HEADS = 16
KERNEL = 31
LENGTH = 6144


def shared_query(key):
    return jax.random.normal(jax.random.fold_in(key, 11), (D, D), jnp.float32) * D ** (-0.5)


def draw_query_weight(key, part):
    return jnp.clip(shared_query(key), -8.0, 8.0).astype(jnp.bfloat16)


def draw_key_weight(key, part):
    own_draw = jax.random.normal(jax.random.fold_in(key, 23), (D, D), jnp.float32) * D ** (-0.5)
    return jnp.clip(own_draw, -8.0, 8.0).astype(jnp.bfloat16)


def block_scale(own_key, extent, split, low, largest):
    def one(dim, parts):
        draws = jax.random.uniform(jax.random.fold_in(jax.random.fold_in(own_key, 6), dim), (parts,), jnp.float32, low / len(split), largest / len(split))
        return jnp.repeat(jnp.exp(draws), extent[dim] // parts).reshape((-1,) + (1,) * (len(extent) - dim - 1))

    level = one(*split[0])
    for cut in split[1:]:
        level = level * one(*cut)
    return level


def gaussian(rng, dims, width, bound, shards=(), kind=jnp.bfloat16):
    loudness = block_scale(rng, dims, shards, -0.22, 0.18) if shards else 1.0
    result = jax.random.normal(rng, dims, jnp.float32) * width * loudness
    return jnp.minimum(jnp.maximum(result, -bound), bound).astype(kind)


def setup_inputs(seed: int = 0, part: int = 0) -> dict:
    seeds = jax.random.split(jax.random.key(seed), 10)
    part_keys = jax.random.split(jax.random.fold_in(seeds[9], part), 10)
    frames = gaussian(part_keys[0], (LENGTH, D), 1.0, 6.0, ((0, 32),), jnp.float32)
    attend_gain = jnp.clip(1.0 + 0.15 * jax.random.normal(seeds[1], (D,), jnp.float32), 0.25, 1.75)
    query_weight = draw_query_weight(jax.random.fold_in(seeds[9], 71), part)
    key_weight = draw_key_weight(jax.random.fold_in(seeds[9], 71), part)
    value_weight = gaussian(seeds[4], (D, D), D ** -0.5, 0.1875)
    output_weight = gaussian(seeds[5], (D, D), D ** -0.5, 0.1875)
    mixer_gain = jnp.clip(1.0 + 0.15 * jax.random.normal(seeds[6], (D,), jnp.float32), 0.25, 1.75)
    depthwise = gaussian(seeds[7], (KERNEL, D), KERNEL ** -0.5, 1.0, (), jnp.float32)
    mixer_bias = gaussian(seeds[8], (D,), 0.5, 3.0, (), jnp.float32)
    return {"frames": frames, "attend_gain": attend_gain, "query_weight": query_weight, "key_weight": key_weight, "value_weight": value_weight, "output_weight": output_weight, "mixer_gain": mixer_gain, "depthwise": depthwise, "mixer_bias": mixer_bias}


def norm_rows(values_in, gain):
    center = lax.optimization_barrier(jnp.mean(values_in, axis=1, keepdims=True))
    spread = lax.optimization_barrier(jnp.mean(jnp.square(values_in - center), axis=1, keepdims=True))
    return (values_in - center) * lax.rsqrt(spread + 1e-05) * gain

def reference(frames, attend_gain, query_weight, key_weight, value_weight, output_weight, mixer_gain, depthwise, mixer_bias):
    normed = norm_rows(frames, attend_gain).astype(jnp.bfloat16)
    query_rows = jnp.dot(normed, query_weight, preferred_element_type=jnp.float32).astype(jnp.bfloat16)
    key_rows = jnp.dot(normed, key_weight, preferred_element_type=jnp.float32).astype(jnp.bfloat16)
    value_rows = jnp.dot(normed, value_weight, preferred_element_type=jnp.float32).astype(jnp.bfloat16)
    head_size = D // HEADS
    score_scale = head_size ** (-0.5)

    def one_head(head):
        column = (head * head_size).astype(jnp.int32)
        query_part = lax.dynamic_slice_in_dim(query_rows, column, head_size, 1)
        key_part = lax.dynamic_slice_in_dim(key_rows, column, head_size, 1)
        value_part = lax.dynamic_slice_in_dim(value_rows, column, head_size, 1)
        scores = lax.dot_general(query_part, key_part, (((1,), (1,)), ((), ())), preferred_element_type=jnp.float32) * score_scale
        highest = lax.optimization_barrier(jnp.max(scores, axis=1, keepdims=True))
        weights = jnp.exp(scores - highest)
        numerator = jnp.dot(weights.astype(jnp.bfloat16), value_part, preferred_element_type=jnp.float32)
        return numerator / lax.optimization_barrier(jnp.sum(weights, axis=1, keepdims=True))
    per_head = lax.map(one_head, jnp.arange(HEADS, dtype=jnp.int32))
    context = jnp.transpose(per_head, (1, 0, 2)).reshape(LENGTH, D).astype(jnp.bfloat16)
    attended = frames + jnp.dot(context, output_weight, preferred_element_type=jnp.float32)
    mixer_in = norm_rows(attended, mixer_gain)
    half_width = KERNEL // 2
    padded = jnp.pad(mixer_in, ((half_width, half_width), (0, 0)))
    convolved = jnp.zeros_like(mixer_in) + mixer_bias
    for tap_index in range(KERNEL):
        convolved = convolved + padded[tap_index:tap_index + LENGTH] * depthwise[tap_index]
    return attended + jax.nn.silu(convolved)
```

```python
import functools
import math

import jax
import jax.numpy as jnp
from jax import lax
from jax.experimental import pallas as pl
from jax.experimental.pallas import tpu as pltpu
from jax.sharding import PartitionSpec as P

F32, BF16 = jnp.float32, jnp.bfloat16
MESH = pl.DeviceIdType.MESH
HEADS = 16
HEAD = 64
KERNEL = 31
ROWS = 192
HALF = ROWS // 2
D = 1024
CHIPS = 16
EDGE = 16
BQ = 4 * ROWS
BK = 8 * ROWS
SCALE = HEAD**-0.5 * math.log2(math.e)
OFFSETS = (
    (0, 0), (0, 1), (0, 7), (1, 0),
    (0, 2), (0, 6), (1, 1), (1, 7),
    (0, 3), (0, 5), (1, 2), (1, 6),
    (0, 4), (1, 3), (1, 5), (1, 4),
)


def rows_at(index, size):
    return pl.ds(pl.multiple_of(index * size, size), size)


def norm(values, gain):
    center = jnp.mean(values, axis=1, keepdims=True)
    spread = jnp.mean(jnp.square(values - center), axis=1, keepdims=True)
    return (values - center) * lax.rsqrt(spread + 1e-05) * gain


def low_lanes(shape):
    return lax.broadcasted_iota(jnp.int32, shape, 1) < HEAD


def swap(values):
    return pltpu.roll(values, HEAD, 1)


def kernel(
    frames_hbm, again_ref, wq_hbm, wk_hbm, wv_hbm, wo_hbm, mgain_ref, taps_ref, bias_ref,
    out_ref,
    frames, wq, wk, wv, wo, normed,
    sendq, sendkv, qbuf, kvbuf, qx, vx, m_ref, o_ref, sendc, cbuf, context, attended, padded,
    load_sem, own_sem, q_send, q_recv, kv_send, kv_recv, f_send, f_recv, c_send, c_recv, h_send, h_recv,
):
    ctx = lax.axis_index("ctx")
    core = lax.rem(ctx, 2)
    chip = ctx // 2
    z, xh = lax.rem(chip, 8), chip // 8
    partner = chip * 2 + 1 - core

    def toward(r):
        dx, dz = OFFSETS[r]
        return lax.rem(xh + dx, 2) * 8 + lax.rem(z + dz, 8)

    def behind(r):
        dx, dz = OFFSETS[r]
        return lax.rem(xh + dx, 2) * 8 + lax.rem(z + 8 - dz, 8)

    def remote(src, dst, send, recv, target):
        return pltpu.make_async_remote_copy(
            src_ref=src, dst_ref=dst, send_sem=send, recv_sem=recv, device_id={"ctx": target}, device_id_type=MESH
        )

    loads = [
        pltpu.make_async_copy(src, dst, load_sem.at[n])
        for n, (src, dst) in enumerate(
            ((frames_hbm, frames), (wq_hbm, wq), (wk_hbm, wk), (wv_hbm, wv), (wo_hbm, wo))
        )
    ]
    for load in loads:
        load.start()

    barrier = pltpu.get_barrier_semaphore()
    greeted = [toward(r) * 2 + core for r in range(1, CHIPS)]
    greeted += [partner, lax.rem(ctx + 31 + 2 * core, 32)]
    for device in greeted:
        pl.semaphore_signal(barrier, inc=1, device_id={"ctx": device}, device_id_type=MESH)

    loads[0].wait()
    normed[...] = norm(frames[...], again_ref[...]).astype(BF16)
    low = low_lanes((ROWS, 128))
    low_half = low_lanes((HALF, 128))
    loads[1].wait()

    def project_q(g, carry):
        cols = rows_at(g, 256)
        q = jnp.dot(normed[...], wq[:, cols], preferred_element_type=F32)
        for pair in range(2):
            piece = q[:, pair * 128 : pair * 128 + 128]
            top, bottom = piece[:HALF], piece[HALF:]
            sendq[4 * g + 2 * pair] = jnp.where(low_half, top, swap(bottom)).astype(BF16)
            sendq[4 * g + 2 * pair + 1] = jnp.where(low_half, swap(top), bottom).astype(BF16)
        return carry

    lax.fori_loop(0, 4, project_q, 0)
    loads[2].wait()
    loads[3].wait()

    def project_kv(g, carry):
        cols = rows_at(g, 256)
        k = jnp.dot(normed[...], wk[:, cols], preferred_element_type=F32)
        v = jnp.dot(normed[...], wv[:, cols], preferred_element_type=F32)
        for pair in range(2):
            kp, vp = k[:, pair * 128 : pair * 128 + 128], v[:, pair * 128 : pair * 128 + 128]
            sendkv[4 * g + 2 * pair] = jnp.where(low, kp, swap(vp)).astype(BF16)
            sendkv[4 * g + 2 * pair + 1] = jnp.where(low, swap(kp), vp).astype(BF16)
        return carry

    lax.fori_loop(0, 4, project_kv, 0)

    def reset(n, carry):
        m_ref[rows_at(n, BQ), :] = jnp.full((BQ, 128), -jnp.inf, F32)
        o_ref[rows_at(n, BQ), :] = jnp.zeros((BQ, 128), F32)
        return carry

    lax.fori_loop(0, CHIPS * ROWS // BQ, reset, 0)
    pl.semaphore_wait(barrier, len(greeted))

    def q_copy(r):
        p = toward(r)
        return remote(sendq.at[p], qbuf.at[r], q_send.at[r], q_recv.at[r], p * 2 + core)

    def kv_rows(slot, which):
        return pl.ds(pl.multiple_of((slot * 2 + which) * ROWS, ROWS), ROWS)

    def kv_copy(r):
        p = toward(r)
        return remote(sendkv.at[p], kvbuf.at[kv_rows(r, core)], kv_send.at[r], kv_recv.at[r], p * 2 + core)

    own_q = pltpu.make_async_copy(sendq.at[chip], qbuf.at[0], own_sem.at[0])
    own_kv = pltpu.make_async_copy(sendkv.at[chip], kvbuf.at[kv_rows(0, core)], own_sem.at[1])
    own_forward = remote(sendkv.at[chip], kvbuf.at[kv_rows(0, core)], f_send.at[0], f_recv.at[0], partner)
    own_q.start()
    own_kv.start()
    own_forward.start()
    q_copies, kv_copies = [None] * CHIPS, [None] * CHIPS
    order = [("q", r) for r in range(1, 4)] + [("kv", r) for r in range(1, 4)]
    order += [("q", r) for r in range(4, CHIPS)] + [("kv", r) for r in range(4, CHIPS)]
    for kind, r in order:
        copy = q_copy(r) if kind == "q" else kv_copy(r)
        copy.start()
        (q_copies if kind == "q" else kv_copies)[r] = copy

    def q_arrival(slot):
        return remote(sendq.at[0], qbuf.at[slot], q_send.at[slot], q_recv.at[slot], partner)

    def kv_arrival(slot):
        return remote(sendkv.at[0], kvbuf.at[kv_rows(slot, core)], kv_send.at[slot], kv_recv.at[slot], partner)

    def forward(slot):
        mine = kvbuf.at[kv_rows(slot, core)]
        return remote(mine, mine, f_send.at[slot], f_recv.at[slot], partner)

    def forwarded(slot):
        theirs = kvbuf.at[kv_rows(slot, 1 - core)]
        return remote(theirs, theirs, f_send.at[slot], f_recv.at[slot], partner)

    own_q.wait()
    own_kv.wait()
    for r in range(1, 4):
        kv_arrival(r).wait_recv()
        forward(r).start()

    def unpack_q(slot):
        x = qbuf[slot].astype(F32)
        at = pl.multiple_of(slot * ROWS, ROWS)
        qx[pl.ds(at, HALF), :] = jnp.where(low_half, x, 0.0).astype(BF16)
        qx[pl.ds(at + HALF, HALF), :] = jnp.where(low_half, swap(x), 0.0).astype(BF16)

    low_wide = low_lanes((2 * ROWS, 128))

    def attend(t, carry):
        j, turn = t // 4, lax.rem(t, 4)
        i = jnp.where(j == 3, 3 - turn, turn)

        @pl.when(j == 0)
        def _():
            for s in range(4):
                @pl.when(i * 4 + s > 0)
                def _():
                    q_arrival(i * 4 + s).wait_recv()
                unpack_q(i * 4 + s)

        @pl.when(turn == 0)
        def _():
            for s in range(4):
                slot = j * 4 + s
                forwarded(slot).wait_recv()
                at = rows_at(slot, 2 * ROWS)
                x = kvbuf[at, :]
                vx[at, :] = jnp.where(low_wide, jnp.ones_like(x), x)

        @pl.when((turn == 3) & (j < 3))
        def _():
            for s in range(4):
                slot = j * 4 + 4 + s
                kv_arrival(slot).wait_recv()
                forward(slot).start()

        q = qx[rows_at(i, BQ), :]
        scores = lax.dot_general(
            q, kvbuf[rows_at(j, BK), :], (((1,), (1,)), ((), ())), preferred_element_type=F32
        )
        old = m_ref[rows_at(i, BQ), :]
        new = jnp.maximum(old, jnp.max(scores, axis=1, keepdims=True))
        weights = jnp.exp2((scores - jnp.concatenate([new] * (BK // 128), axis=1)) * SCALE).astype(BF16)
        part = jnp.dot(weights, vx[rows_at(j, BK), :], preferred_element_type=F32)
        o_ref[rows_at(i, BQ), :] = o_ref[rows_at(i, BQ), :] * jnp.exp2((old - new) * SCALE) + part
        m_ref[rows_at(i, BQ), :] = new

        @pl.when(j == 3)
        def _():
            for s in range(4):
                o = o_ref[rows_at(i * 4 + s, ROWS), :]
                c = o / swap(o)
                sendc[i * 4 + s] = jnp.where(low_half, swap(c[:HALF]), c[HALF:]).astype(BF16)
            for block in range(4):
                @pl.when(i == block)
                def _():
                    for r in range(block * 4, block * 4 + 4):
                        if r > 0:
                            remote(sendc.at[r], cbuf.at[chip], c_send.at[r], c_recv.at[r], behind(r) * 2 + core).start()

        return carry

    lax.fori_loop(0, 16, attend, 0)

    own_c = pltpu.make_async_copy(sendc.at[0], cbuf.at[chip], own_sem.at[2])
    own_c.start()
    loads[4].wait()
    own_c.wait()
    for r in range(1, CHIPS):
        remote(sendc.at[r], cbuf.at[toward(r)], c_send.at[r], c_recv.at[r], partner).wait_recv()
    for pair in range(HEADS // 2):
        a, b = cbuf[2 * pair].astype(F32), cbuf[2 * pair + 1].astype(F32)
        cols = slice(pair * 128, pair * 128 + 128)
        context[:HALF, cols] = jnp.where(low_half, a, swap(b)).astype(BF16)
        context[HALF:, cols] = jnp.where(low_half, swap(a), b).astype(BF16)
    attended[...] = frames[...] + jnp.dot(context[...], wo[...], preferred_element_type=F32)
    mixer_in = norm(attended[...], mgain_ref[...])
    for n in range(8):
        padded[n, EDGE : EDGE + ROWS, :] = mixer_in[:, n * 128 : n * 128 + 128]

    after, before = lax.rem(ctx + 1, 32), lax.rem(ctx + 31, 32)
    up = remote(
        padded.at[:, pl.ds(ROWS, EDGE)], padded.at[:, pl.ds(0, EDGE)], h_send.at[0], h_recv.at[0], after
    )
    down = remote(
        padded.at[:, pl.ds(EDGE, EDGE)], padded.at[:, pl.ds(EDGE + ROWS, EDGE)], h_send.at[1], h_recv.at[1], before
    )
    up.start()
    down.start()

    def convolve(first, count, above=None, below=None):
        def column(n, carry):
            lanes = rows_at(n, 128)
            weights = taps_ref[:, lanes]
            bias = bias_ref[:, lanes]
            for at in range(first, first + count, 8):
                total = jnp.broadcast_to(bias, (8, 128))
                for tap in range(KERNEL):
                    total = total + padded[n, at + tap + 1 : at + tap + 9, :] * weights[tap : tap + 1, :]
                out_ref[at : at + 8, lanes] = attended[at : at + 8, lanes] + total / (1.0 + jnp.exp(-total))
            return carry

        lax.fori_loop(0, 8, column, 0)

    convolve(EDGE, ROWS - 2 * EDGE)
    up.wait()
    down.wait()

    @pl.when(ctx == 0)
    def _():
        padded[:, :EDGE, :] = jnp.zeros((8, EDGE, 128), F32)

    @pl.when(ctx == 31)
    def _():
        padded[:, EDGE + ROWS :, :] = jnp.zeros((8, EDGE, 128), F32)

    convolve(0, EDGE)
    convolve(ROWS - EDGE, EDGE)

    own_forward.wait_send()
    for r in range(1, CHIPS):
        q_copies[r].wait_send()
        kv_copies[r].wait_send()
        forward(r).wait_send()
        remote(sendc.at[r], cbuf.at[chip], c_send.at[r], c_recv.at[r], partner).wait_send()


def per_device(frames, attend_gain, wq, wk, wv, wo, mixer_gain, depthwise, mixer_bias):
    hbm = pl.BlockSpec(memory_space=pl.ANY)
    vmem = pl.BlockSpec(memory_space=pltpu.VMEM)
    dma = pltpu.SemaphoreType.DMA
    return pl.pallas_call(
        kernel,
        out_shape=jax.ShapeDtypeStruct((ROWS, D), F32),
        in_specs=[hbm, vmem, hbm, hbm, hbm, hbm, vmem, vmem, vmem],
        out_specs=vmem,
        scratch_shapes=[
            pltpu.VMEM((ROWS, D), F32),
            *[pltpu.VMEM((D, D), BF16)] * 4,
            pltpu.VMEM((ROWS, D), BF16),
            pltpu.VMEM((HEADS, HALF, 128), BF16),
            pltpu.VMEM((HEADS, ROWS, 128), BF16),
            pltpu.VMEM((CHIPS, HALF, 128), BF16),
            pltpu.VMEM((CHIPS * 2 * ROWS, 128), BF16),
            pltpu.VMEM((CHIPS * ROWS, 128), BF16),
            pltpu.VMEM((CHIPS * 2 * ROWS, 128), BF16),
            pltpu.VMEM((CHIPS * ROWS, 128), F32),
            pltpu.VMEM((CHIPS * ROWS, 128), F32),
            pltpu.VMEM((CHIPS, HALF, 128), BF16),
            pltpu.VMEM((HEADS, HALF, 128), BF16),
            pltpu.VMEM((ROWS, D), BF16),
            pltpu.VMEM((ROWS, D), F32),
            pltpu.VMEM((8, ROWS + 2 * EDGE, 128), F32),
            dma((5,)), dma((3,)),
            *[dma((CHIPS,))] * 8,
            dma((2,)), dma((2,)),
        ],
        compiler_params=pltpu.CompilerParams(
            collective_id=0, has_side_effects=True, vmem_limit_bytes=60 * 1024 * 1024
        ),
        name="block",
    )(
        frames, attend_gain.reshape(1, D), wq, wk, wv, wo,
        mixer_gain.reshape(1, D), depthwise, mixer_bias.reshape(1, D),
    )


def solution(mesh):
    in_specs = (P(("session", "ctx"), None), P(), P(), P(), P(), P(), P(), P(), P())
    return jax.shard_map(
        per_device, mesh=mesh, in_specs=in_specs, out_specs=P(("session", "ctx"), None), check_vma=False
    )
```

```python
import functools
import math

import jax
import jax.numpy as jnp
from jax import lax
from jax.experimental import pallas as pl
from jax.experimental.pallas import tpu as pltpu
from jax.sharding import PartitionSpec as P

F32, BF16 = jnp.float32, jnp.bfloat16
MESH = pl.DeviceIdType.MESH
HEADS = 16
HEAD = 64
KERNEL = 31
ROWS = 192
HALF = ROWS // 2
D = 1024
CHIPS = 16
EDGE = 16
BQ = 4 * ROWS
GRANT = 48 * 1024 * 1024
BK = 8 * ROWS
SCALE = HEAD**-0.5 * math.log2(math.e)
OFFSETS = (
    (0, 0), (0, 1), (0, 7), (1, 0),
    (0, 2), (0, 6), (1, 1), (1, 7),
    (0, 3), (0, 5), (1, 2), (1, 6),
    (0, 4), (1, 3), (1, 5), (1, 4),
)


def rows_at(index, size):
    return pl.ds(pl.multiple_of(index * size, size), size)


def norm(values, gain):
    center = jnp.mean(values, axis=1, keepdims=True)
    spread = jnp.mean(jnp.square(values - center), axis=1, keepdims=True)
    return (values - center) * lax.rsqrt(spread + 1e-05) * gain


def low_lanes(shape):
    return lax.broadcasted_iota(jnp.int32, shape, 1) < HEAD


def swap(values):
    return pltpu.roll(values, HEAD, 1)


def kernel(
    frames_hbm, again_hbm, wq_hbm, wk_hbm, wv_hbm, wo_hbm, mgain_hbm,
    padded, attended,
    frames, again_ref, wq, wk, wv, wo, mgain_ref, normed,
    sendq, sendkv, qbuf, kvbuf, qx, vx, m_ref, o_ref, sendc, cbuf, context, edges, halos,
    load_sem, own_sem, q_send, q_recv, kv_send, kv_recv, f_send, f_recv, c_send, c_recv, h_send, h_recv,
):
    ctx = lax.axis_index("ctx")
    core = lax.rem(ctx, 2)
    chip = ctx // 2
    z, xh = lax.rem(chip, 8), chip // 8
    partner = chip * 2 + 1 - core

    def toward(r):
        dx, dz = OFFSETS[r]
        return lax.rem(xh + dx, 2) * 8 + lax.rem(z + dz, 8)

    def behind(r):
        dx, dz = OFFSETS[r]
        return lax.rem(xh + dx, 2) * 8 + lax.rem(z + 8 - dz, 8)

    def remote(src, dst, send, recv, target):
        return pltpu.make_async_remote_copy(
            src_ref=src, dst_ref=dst, send_sem=send, recv_sem=recv, device_id={"ctx": target}, device_id_type=MESH
        )
    loads = [
        pltpu.make_async_copy(src, dst, load_sem.at[n])
        for n, (src, dst) in enumerate(
            (
                (frames_hbm, frames), (again_hbm, again_ref), (wq_hbm, wq), (wk_hbm, wk),
                (wv_hbm, wv), (wo_hbm, wo), (mgain_hbm, mgain_ref),
            )
        )
    ]
    for load in loads:
        load.start()

    barrier = pltpu.get_barrier_semaphore()
    greeted = [toward(r) * 2 + core for r in range(1, CHIPS)]
    greeted += [partner, lax.rem(ctx + 31 + 2 * core, 32)]
    for device in greeted:
        pl.semaphore_signal(barrier, inc=1, device_id={"ctx": device}, device_id_type=MESH)

    loads[0].wait()
    loads[1].wait()
    normed[...] = norm(frames[...], again_ref[...]).astype(BF16)
    low = low_lanes((ROWS, 128))
    low_half = low_lanes((HALF, 128))
    loads[2].wait()
    for g in range(4):
        q = jnp.dot(normed[...], wq[:, g * 256 : g * 256 + 256], preferred_element_type=F32)
        for pair in range(2):
            piece = q[:, pair * 128 : pair * 128 + 128]
            top, bottom = piece[:HALF], piece[HALF:]
            sendq[4 * g + 2 * pair] = jnp.where(low_half, top, swap(bottom)).astype(BF16)
            sendq[4 * g + 2 * pair + 1] = jnp.where(low_half, swap(top), bottom).astype(BF16)

    def q_copy(r):
        p = toward(r)
        return remote(sendq.at[p], qbuf.at[r], q_send.at[r], q_recv.at[r], p * 2 + core)

    def kv_rows(slot, which):
        return pl.ds(pl.multiple_of((slot * 2 + which) * ROWS, ROWS), ROWS)

    def kv_copy(r):
        p = toward(r)
        return remote(sendkv.at[p], kvbuf.at[kv_rows(r, core)], kv_send.at[r], kv_recv.at[r], p * 2 + core)

    q_copies, kv_copies = [None] * CHIPS, [None] * CHIPS

    def send(order):
        for kind, r in order:
            copy = q_copy(r) if kind == "q" else kv_copy(r)
            copy.start()
            (q_copies if kind == "q" else kv_copies)[r] = copy

    own_q = pltpu.make_async_copy(sendq.at[chip], qbuf.at[0], own_sem.at[0])
    own_q.start()
    pl.semaphore_wait(barrier, len(greeted))
    send([("q", r) for r in range(1, 8)])
    loads[3].wait()
    loads[4].wait()
    for g in range(4):
        k = jnp.dot(normed[...], wk[:, g * 256 : g * 256 + 256], preferred_element_type=F32)
        v = jnp.dot(normed[...], wv[:, g * 256 : g * 256 + 256], preferred_element_type=F32)
        for pair in range(2):
            kp, vp = k[:, pair * 128 : pair * 128 + 128], v[:, pair * 128 : pair * 128 + 128]
            sendkv[4 * g + 2 * pair] = jnp.where(low, kp, swap(vp)).astype(BF16)
            sendkv[4 * g + 2 * pair + 1] = jnp.where(low, swap(kp), vp).astype(BF16)
    own_kv = pltpu.make_async_copy(sendkv.at[chip], kvbuf.at[kv_rows(0, core)], own_sem.at[1])
    own_forward = remote(sendkv.at[chip], kvbuf.at[kv_rows(0, core)], f_send.at[0], f_recv.at[0], partner)
    own_kv.start()
    own_forward.start()
    send([("kv", r) for r in range(1, 4)] + [("q", r) for r in range(8, CHIPS)] + [("kv", r) for r in range(4, CHIPS)])

    def reset(n, carry):
        m_ref[rows_at(n, BQ), :] = jnp.full((BQ, 128), -jnp.inf, F32)
        o_ref[rows_at(n, BQ), :] = jnp.zeros((BQ, 128), F32)
        return carry

    lax.fori_loop(0, CHIPS * ROWS // BQ, reset, 0)
    def q_arrival(slot):
        return remote(sendq.at[0], qbuf.at[slot], q_send.at[slot], q_recv.at[slot], partner)

    def kv_arrival(slot):
        return remote(sendkv.at[0], kvbuf.at[kv_rows(slot, core)], kv_send.at[slot], kv_recv.at[slot], partner)

    def forward(slot):
        mine = kvbuf.at[kv_rows(slot, core)]
        return remote(mine, mine, f_send.at[slot], f_recv.at[slot], partner)

    def forwarded(slot):
        theirs = kvbuf.at[kv_rows(slot, 1 - core)]
        return remote(theirs, theirs, f_send.at[slot], f_recv.at[slot], partner)
    own_q.wait()
    own_kv.wait()
    for r in range(1, 4):
        kv_arrival(r).wait_recv()
        forward(r).start()

    def unpack_q(slot):
        x = qbuf[slot].astype(F32)
        at = pl.multiple_of(slot * ROWS, ROWS)
        qx[pl.ds(at, HALF), :] = jnp.where(low_half, x, 0.0).astype(BF16)
        qx[pl.ds(at + HALF, HALF), :] = jnp.where(low_half, swap(x), 0.0).astype(BF16)

    low_wide = low_lanes((2 * ROWS, 128))

    def attend(t, carry):
        j, turn = t // 4, lax.rem(t, 4)
        i = jnp.where(j == 3, 3 - turn, turn)
        @pl.when(j == 0)
        def _():
            for s in range(4):
                @pl.when(i * 4 + s > 0)
                def _():
                    q_arrival(i * 4 + s).wait_recv()
                unpack_q(i * 4 + s)
        @pl.when(turn == 0)
        def _():
            for s in range(4):
                slot = j * 4 + s
                forwarded(slot).wait_recv()
                at = rows_at(slot, 2 * ROWS)
                x = kvbuf[at, :]
                vx[at, :] = jnp.where(low_wide, jnp.ones_like(x), x)
        @pl.when((turn == 3) & (j < 3))
        def _():
            for s in range(4):
                slot = j * 4 + 4 + s
                kv_arrival(slot).wait_recv()
                forward(slot).start()
        q = qx[rows_at(i, BQ), :]
        scores = lax.dot_general(
            q, kvbuf[rows_at(j, BK), :], (((1,), (1,)), ((), ())), preferred_element_type=F32
        )
        old = m_ref[rows_at(i, BQ), :]
        new = jnp.maximum(old, jnp.max(scores, axis=1, keepdims=True))
        weights = jnp.exp2((scores - jnp.concatenate([new] * (BK // 128), axis=1)) * SCALE).astype(BF16)
        part = jnp.dot(weights, vx[rows_at(j, BK), :], preferred_element_type=F32)
        o_ref[rows_at(i, BQ), :] = o_ref[rows_at(i, BQ), :] * jnp.exp2((old - new) * SCALE) + part
        m_ref[rows_at(i, BQ), :] = new
        @pl.when(j == 3)
        def _():
            for s in range(4):
                o = o_ref[rows_at(i * 4 + s, ROWS), :]
                c = o / swap(o)
                sendc[i * 4 + s] = jnp.where(low_half, swap(c[:HALF]), c[HALF:]).astype(BF16)
            for block in range(4):
                @pl.when(i == block)
                def _():
                    for r in range(block * 4, block * 4 + 4):
                        if r > 0:
                            remote(sendc.at[r], cbuf.at[chip], c_send.at[r], c_recv.at[r], behind(r) * 2 + core).start()

        return carry
    lax.fori_loop(0, 16, attend, 0)

    own_c = pltpu.make_async_copy(sendc.at[0], cbuf.at[chip], own_sem.at[2])
    own_c.start()
    loads[5].wait()
    loads[6].wait()
    own_c.wait()
    for r in range(1, CHIPS):
        remote(sendc.at[r], cbuf.at[toward(r)], c_send.at[r], c_recv.at[r], partner).wait_recv()
    for pair in range(HEADS // 2):
        a, b = cbuf[2 * pair].astype(F32), cbuf[2 * pair + 1].astype(F32)
        cols = slice(pair * 128, pair * 128 + 128)
        context[:HALF, cols] = jnp.where(low_half, a, swap(b)).astype(BF16)
        context[HALF:, cols] = jnp.where(low_half, swap(a), b).astype(BF16)
    total = frames[...] + jnp.dot(context[...], wo[...], preferred_element_type=F32)
    mixer_in = norm(total, mgain_ref[...])
    for n in range(8):
        part = mixer_in[:, n * 128 : n * 128 + 128]
        edges[0, n] = part[:EDGE]
        edges[1, n] = part[ROWS - EDGE :]
        padded[n, EDGE : EDGE + ROWS, :] = part
        attended[n] = total[:, n * 128 : n * 128 + 128]

    after, before = lax.rem(ctx + 1, 32), lax.rem(ctx + 31, 32)
    up = remote(edges.at[1], halos.at[0], h_send.at[0], h_recv.at[0], after)
    down = remote(edges.at[0], halos.at[1], h_send.at[1], h_recv.at[1], before)
    up.start()
    down.start()
    up.wait()
    down.wait()
    padded[:, :EDGE, :] = jnp.where(ctx > 0, halos[0], 0.0)
    padded[:, EDGE + ROWS :, :] = jnp.where(ctx < 31, halos[1], 0.0)
    own_forward.wait_send()
    for r in range(1, CHIPS):
        q_copies[r].wait_send()
        kv_copies[r].wait_send()
        forward(r).wait_send()
        remote(sendc.at[r], cbuf.at[chip], c_send.at[r], c_recv.at[r], partner).wait_send()


def convolve(padded_ref, attended_ref, taps_ref, bias_ref, out_hbm, result, sems):
    def copy(n):
        return pltpu.make_async_copy(result.at[n], out_hbm.at[:, rows_at(n, 128)], sems.at[n])

    def column(n, carry):
        lanes = rows_at(n, 128)
        taps = taps_ref[:, lanes]
        bias = jnp.broadcast_to(bias_ref[:, lanes], (8, 128))
        for at in range(0, ROWS, 8):
            total = bias
            for tap in range(KERNEL):
                total = total + padded_ref[n, at + tap + 1 : at + tap + 9, :] * taps[tap : tap + 1, :]
            result[n, at : at + 8, :] = attended_ref[n, at : at + 8, :] + total / (1.0 + jnp.exp(-total))
        copy(n).start()
        return carry

    lax.fori_loop(0, 8, column, 0)
    for n in range(8):
        copy(n).wait()


def per_device(frames, attend_gain, wq, wk, wv, wo, mixer_gain, depthwise, mixer_bias):
    hbm = pl.BlockSpec(memory_space=pltpu.HBM)
    vmem = pl.BlockSpec(memory_space=pltpu.VMEM)
    dma = pltpu.SemaphoreType.DMA
    padded, attended = pl.pallas_call(
        kernel,
        out_shape=(
            jax.ShapeDtypeStruct((8, ROWS + 2 * EDGE, 128), F32),
            jax.ShapeDtypeStruct((8, ROWS, 128), F32),
        ),
        in_specs=[hbm] * 7,
        out_specs=(vmem, vmem),
        scratch_shapes=[
            pltpu.VMEM((ROWS, D), F32),
            pltpu.VMEM((1, D), F32),
            *[pltpu.VMEM((D, D), BF16)] * 4,
            pltpu.VMEM((1, D), F32),
            pltpu.VMEM((ROWS, D), BF16),
            pltpu.VMEM((HEADS, HALF, 128), BF16),
            pltpu.VMEM((HEADS, ROWS, 128), BF16),
            pltpu.VMEM((CHIPS, HALF, 128), BF16),
            pltpu.VMEM((CHIPS * 2 * ROWS, 128), BF16),
            pltpu.VMEM((CHIPS * ROWS, 128), BF16),
            pltpu.VMEM((CHIPS * 2 * ROWS, 128), BF16),
            pltpu.VMEM((CHIPS * ROWS, 128), F32),
            pltpu.VMEM((CHIPS * ROWS, 128), F32),
            pltpu.VMEM((CHIPS, HALF, 128), BF16),
            pltpu.VMEM((HEADS, HALF, 128), BF16),
            pltpu.VMEM((ROWS, D), BF16),
            pltpu.VMEM((2, 8, EDGE, 128), F32),
            pltpu.VMEM((2, 8, EDGE, 128), F32),
            dma((7,)), dma((3,)),
            *[dma((CHIPS,))] * 8,
            dma((2,)), dma((2,)),
        ],
        compiler_params=pltpu.CompilerParams(
            collective_id=0, has_side_effects=True, vmem_limit_bytes=GRANT
        ),
        name="block",
    )(*(pltpu.with_memory_space_constraint(a, pltpu.HBM) for a in (frames, attend_gain.reshape(1, D), wq, wk, wv, wo, mixer_gain.reshape(1, D))))
    return pl.pallas_call(
        convolve,
        out_shape=jax.ShapeDtypeStruct((ROWS, D), F32),
        in_specs=[vmem] * 4,
        out_specs=hbm,
        scratch_shapes=[pltpu.VMEM((8, ROWS, 128), F32), dma((8,))],
        compiler_params=pltpu.CompilerParams(vmem_limit_bytes=16 * 1024 * 1024),
        name="convolve",
    )(padded, attended, depthwise, mixer_bias.reshape(1, D))


def solution(mesh):
    in_specs = (P(("session", "ctx"), None), P(), P(), P(), P(), P(), P(), P(), P())
    return jax.shard_map(
        per_device, mesh=mesh, in_specs=in_specs, out_specs=P(("session", "ctx"), None), check_vma=False
    )
```

```python
import functools
import math

import jax
import jax.numpy as jnp
from jax import lax
from jax.experimental import pallas as pl
from jax.experimental.pallas import tpu as pltpu
from jax.sharding import PartitionSpec as P

F32, BF16 = jnp.float32, jnp.bfloat16
MESH = pl.DeviceIdType.MESH
HEADS = 16
HEAD = 64
KERNEL = 31
ROWS = 192
HALF = ROWS // 2
D = 1024
CHIPS = 16
EDGE = 16
BQ = 4 * ROWS
GRANT = 48 * 1024 * 1024
BK = 8 * ROWS
SCALE = HEAD**-0.5 * math.log2(math.e)
OFFSETS = (
    (0, 0), (0, 1), (0, 7), (1, 0),
    (0, 2), (0, 6), (1, 1), (1, 7),
    (0, 3), (0, 5), (1, 2), (1, 6),
    (0, 4), (1, 3), (1, 5), (1, 4),
)


QUERY_BLOCKS = (0, 1, 0, 1, 2, 2, 3, 3, 3, 2, 3, 2, 1, 1, 0, 0)
KEY_CHUNKS = (0, 0, 1, 1, 0, 1, 0, 1, 2, 2, 3, 3, 2, 3, 2, 3)


def pick(step, table):
    value = jnp.int32(table[0])
    for n in range(1, len(table)):
        if table[n] != table[0]:
            value = jnp.where(step == n, table[n], value)
    return value


def first(step, table):
    steps = [table.index(value) for value in range(4)]
    return functools.reduce(jnp.logical_or, [step == n for n in steps])


def rows_at(index, size):
    return pl.ds(pl.multiple_of(index * size, size), size)


def norm(values, gain):
    center = jnp.mean(values, axis=1, keepdims=True)
    spread = jnp.mean(jnp.square(values - center), axis=1, keepdims=True)
    return (values - center) * lax.rsqrt(spread + 1e-05) * gain


def low_lanes(shape):
    return lax.broadcasted_iota(jnp.int32, shape, 1) < HEAD


def swap(values):
    return pltpu.roll(values, HEAD, 1)


def mix(n, starts, padded, attended, taps_ref, bias_ref, out, shift):
    lanes = rows_at(n, 128)
    taps = taps_ref[:, lanes]
    bias = jnp.broadcast_to(bias_ref[:, lanes], (8, 128))
    for at in starts:
        total = bias
        for tap in range(KERNEL):
            total = total + padded[n, at + tap + 1 : at + tap + 9, :] * taps[tap : tap + 1, :]
        out[n, at - shift : at - shift + 8, :] = attended[n, at : at + 8, :] + total / (1.0 + jnp.exp(-total))


def kernel(
    frames_hbm, again_hbm, wq_hbm, wk_hbm, wv_hbm, wo_hbm, mgain_hbm, taps_hbm, bias_hbm,
    padded, mixed,
    frames, again_ref, wq, wk, wv, wo, mgain_ref, normed,
    sendq, sendkv, qbuf, kvbuf, qx, vx, m_ref, o_ref, sendc, cbuf, context, edges, halos, taps_ref, bias_ref,
    load_sem, own_sem, q_send, q_recv, kv_send, kv_recv, f_send, f_recv, c_send, c_recv, h_send, h_recv,
):
    ctx = lax.axis_index("ctx")
    core = lax.rem(ctx, 2)
    chip = ctx // 2
    z, xh = lax.rem(chip, 8), chip // 8
    partner = chip * 2 + 1 - core

    def toward(r):
        dx, dz = OFFSETS[r]
        return lax.rem(xh + dx, 2) * 8 + lax.rem(z + dz, 8)

    def behind(r):
        dx, dz = OFFSETS[r]
        return lax.rem(xh + dx, 2) * 8 + lax.rem(z + 8 - dz, 8)

    def remote(src, dst, send, recv, target):
        return pltpu.make_async_remote_copy(
            src_ref=src, dst_ref=dst, send_sem=send, recv_sem=recv, device_id={"ctx": target}, device_id_type=MESH
        )
    loads = [
        pltpu.make_async_copy(src, dst, load_sem.at[n])
        for n, (src, dst) in enumerate(
            (
                (frames_hbm, frames), (again_hbm, again_ref), (wq_hbm, wq), (wk_hbm, wk),
                (wv_hbm, wv), (wo_hbm, wo), (mgain_hbm, mgain_ref), (taps_hbm, taps_ref), (bias_hbm, bias_ref),
            )
        )
    ]
    for load in loads:
        load.start()

    barrier = pltpu.get_barrier_semaphore()
    greeted = [toward(r) * 2 + core for r in range(1, CHIPS)]
    greeted += [partner, lax.rem(ctx + 31 + 2 * core, 32)]
    for device in greeted:
        pl.semaphore_signal(barrier, inc=1, device_id={"ctx": device}, device_id_type=MESH)

    loads[0].wait()
    loads[1].wait()
    normed[...] = norm(frames[...], again_ref[...]).astype(BF16)
    low = low_lanes((ROWS, 128))
    low_half = low_lanes((HALF, 128))
    loads[2].wait()
    for g in range(4):
        q = jnp.dot(normed[...], wq[:, g * 256 : g * 256 + 256], preferred_element_type=F32)
        for pair in range(2):
            piece = q[:, pair * 128 : pair * 128 + 128]
            top, bottom = piece[:HALF], piece[HALF:]
            sendq[4 * g + 2 * pair] = jnp.where(low_half, top, swap(bottom)).astype(BF16)
            sendq[4 * g + 2 * pair + 1] = jnp.where(low_half, swap(top), bottom).astype(BF16)

    def q_copy(r):
        p = toward(r)
        return remote(sendq.at[p], qbuf.at[r], q_send.at[r], q_recv.at[r], p * 2 + core)

    def kv_rows(slot, which):
        return pl.ds(pl.multiple_of((slot * 2 + which) * ROWS, ROWS), ROWS)

    def kv_copy(r):
        p = toward(r)
        return remote(sendkv.at[p], kvbuf.at[kv_rows(r, core)], kv_send.at[r], kv_recv.at[r], p * 2 + core)

    q_copies, kv_copies = [None] * CHIPS, [None] * CHIPS

    def send(order):
        for kind, r in order:
            copy = q_copy(r) if kind == "q" else kv_copy(r)
            copy.start()
            (q_copies if kind == "q" else kv_copies)[r] = copy

    own_q = pltpu.make_async_copy(sendq.at[chip], qbuf.at[0], own_sem.at[0])
    own_q.start()
    pl.semaphore_wait(barrier, len(greeted))
    send([("q", r) for r in range(1, 8)])
    loads[3].wait()
    loads[4].wait()
    for g in range(4):
        k = jnp.dot(normed[...], wk[:, g * 256 : g * 256 + 256], preferred_element_type=F32)
        v = jnp.dot(normed[...], wv[:, g * 256 : g * 256 + 256], preferred_element_type=F32)
        for pair in range(2):
            kp, vp = k[:, pair * 128 : pair * 128 + 128], v[:, pair * 128 : pair * 128 + 128]
            sendkv[4 * g + 2 * pair] = jnp.where(low, kp, swap(vp)).astype(BF16)
            sendkv[4 * g + 2 * pair + 1] = jnp.where(low, swap(kp), vp).astype(BF16)
    own_kv = pltpu.make_async_copy(sendkv.at[chip], kvbuf.at[kv_rows(0, core)], own_sem.at[1])
    own_forward = remote(sendkv.at[chip], kvbuf.at[kv_rows(0, core)], f_send.at[0], f_recv.at[0], partner)
    own_kv.start()
    own_forward.start()
    send([("kv", r) for r in range(1, 8)] + [("q", r) for r in range(8, CHIPS)] + [("kv", r) for r in range(8, CHIPS)])

    def reset(n, carry):
        m_ref[rows_at(n, BQ), :] = jnp.full((BQ, 128), -jnp.inf, F32)
        o_ref[rows_at(n, BQ), :] = jnp.zeros((BQ, 128), F32)
        return carry

    lax.fori_loop(0, CHIPS * ROWS // BQ, reset, 0)
    def q_arrival(slot):
        return remote(sendq.at[0], qbuf.at[slot], q_send.at[slot], q_recv.at[slot], partner)

    def kv_arrival(slot):
        return remote(sendkv.at[0], kvbuf.at[kv_rows(slot, core)], kv_send.at[slot], kv_recv.at[slot], partner)

    def forward(slot):
        mine = kvbuf.at[kv_rows(slot, core)]
        return remote(mine, mine, f_send.at[slot], f_recv.at[slot], partner)

    def forwarded(slot):
        theirs = kvbuf.at[kv_rows(slot, 1 - core)]
        return remote(theirs, theirs, f_send.at[slot], f_recv.at[slot], partner)
    own_q.wait()
    own_kv.wait()
    for r in range(1, 4):
        kv_arrival(r).wait_recv()
        forward(r).start()

    def unpack_q(slot):
        x = qbuf[slot].astype(F32)
        at = pl.multiple_of(slot * ROWS, ROWS)
        qx[pl.ds(at, HALF), :] = jnp.where(low_half, x, 0.0).astype(BF16)
        qx[pl.ds(at + HALF, HALF), :] = jnp.where(low_half, swap(x), 0.0).astype(BF16)

    low_wide = low_lanes((2 * ROWS, 128))

    def attend(t, carry):
        i, j = pick(t, QUERY_BLOCKS), pick(t, KEY_CHUNKS)
        @pl.when(first(t, QUERY_BLOCKS))
        def _():
            for s in range(4):
                @pl.when(i * 4 + s > 0)
                def _():
                    q_arrival(i * 4 + s).wait_recv()
                unpack_q(i * 4 + s)
        @pl.when(first(t, KEY_CHUNKS))
        def _():
            for s in range(4):
                slot = j * 4 + s
                forwarded(slot).wait_recv()
                at = rows_at(slot, 2 * ROWS)
                x = kvbuf[at, :]
                vx[at, :] = jnp.where(low_wide, jnp.ones_like(x), x)
        @pl.when(first(t + 1, KEY_CHUNKS))
        def _():
            for s in range(4):
                slot = pick(t + 1, KEY_CHUNKS) * 4 + s
                kv_arrival(slot).wait_recv()
                forward(slot).start()
        q = qx[rows_at(i, BQ), :]
        scores = lax.dot_general(
            q, kvbuf[rows_at(j, BK), :], (((1,), (1,)), ((), ())), preferred_element_type=F32
        )
        old = m_ref[rows_at(i, BQ), :]
        new = jnp.maximum(old, jnp.max(scores, axis=1, keepdims=True))
        weights = jnp.exp2((scores - jnp.concatenate([new] * (BK // 128), axis=1)) * SCALE).astype(BF16)
        part = jnp.dot(weights, vx[rows_at(j, BK), :], preferred_element_type=F32)
        o_ref[rows_at(i, BQ), :] = o_ref[rows_at(i, BQ), :] * jnp.exp2((old - new) * SCALE) + part
        m_ref[rows_at(i, BQ), :] = new
        @pl.when(j == 3)
        def _():
            for s in range(4):
                o = o_ref[rows_at(i * 4 + s, ROWS), :]
                c = o / swap(o)
                sendc[i * 4 + s] = jnp.where(low_half, swap(c[:HALF]), c[HALF:]).astype(BF16)
            for block in range(4):
                @pl.when(i == block)
                def _():
                    for r in range(block * 4, block * 4 + 4):
                        if r > 0:
                            remote(sendc.at[r], cbuf.at[chip], c_send.at[r], c_recv.at[r], behind(r) * 2 + core).start()

        return carry
    lax.fori_loop(0, 16, attend, 0)

    own_c = pltpu.make_async_copy(sendc.at[0], cbuf.at[chip], own_sem.at[2])
    own_c.start()
    for load in loads[5:]:
        load.wait()
    own_c.wait()
    for r in range(1, CHIPS):
        remote(sendc.at[r], cbuf.at[toward(r)], c_send.at[r], c_recv.at[r], partner).wait_recv()
    for pair in range(HEADS // 2):
        a, b = cbuf[2 * pair].astype(F32), cbuf[2 * pair + 1].astype(F32)
        cols = slice(pair * 128, pair * 128 + 128)
        context[:HALF, cols] = jnp.where(low_half, a, swap(b)).astype(BF16)
        context[HALF:, cols] = jnp.where(low_half, swap(a), b).astype(BF16)
    total = frames[...] + jnp.dot(context[...], wo[...], preferred_element_type=F32)
    mixer_in = norm(total, mgain_ref[...])
    for n in range(8):
        part = mixer_in[:, n * 128 : n * 128 + 128]
        edges[0, n] = part[:EDGE]
        edges[1, n] = part[ROWS - EDGE :]
        padded[n, EDGE : EDGE + ROWS, :] = part
        mixed[n] = total[:, n * 128 : n * 128 + 128]

    after, before = lax.rem(ctx + 1, 32), lax.rem(ctx + 31, 32)
    up = remote(edges.at[1], halos.at[0], h_send.at[0], h_recv.at[0], after)
    down = remote(edges.at[0], halos.at[1], h_send.at[1], h_recv.at[1], before)
    up.start()
    down.start()

    def interior(n, carry):
        mix(n, range(EDGE, ROWS - EDGE, 8), padded, mixed, taps_ref, bias_ref, mixed, 0)
        return carry

    lax.fori_loop(0, 8, interior, 0)
    up.wait()
    down.wait()
    padded[:, :EDGE, :] = jnp.where(ctx > 0, halos[0], 0.0)
    padded[:, EDGE + ROWS :, :] = jnp.where(ctx < 31, halos[1], 0.0)
    own_forward.wait_send()
    for r in range(1, CHIPS):
        q_copies[r].wait_send()
        kv_copies[r].wait_send()
        forward(r).wait_send()
        remote(sendc.at[r], cbuf.at[chip], c_send.at[r], c_recv.at[r], partner).wait_send()


def convolve(padded_ref, mixed_ref, taps_ref, bias_ref, out_hbm, result, inner_sems, edge_sems):
    def inner(n):
        rows = pl.ds(EDGE, ROWS - 2 * EDGE)
        return pltpu.make_async_copy(mixed_ref.at[n, rows], out_hbm.at[rows, rows_at(n, 128)], inner_sems.at[n])

    def edge(n, side):
        rows = pl.ds(side * (ROWS - EDGE), EDGE)
        return pltpu.make_async_copy(result.at[n, side], out_hbm.at[rows, rows_at(n, 128)], edge_sems.at[n, side])

    for n in range(8):
        inner(n).start()

    def column(n, carry):
        mix(n, range(0, EDGE, 8), padded_ref, mixed_ref, taps_ref, bias_ref, result.at[:, 0], 0)
        mix(n, range(ROWS - EDGE, ROWS, 8), padded_ref, mixed_ref, taps_ref, bias_ref, result.at[:, 1], ROWS - EDGE)
        edge(n, 0).start()
        edge(n, 1).start()
        return carry

    lax.fori_loop(0, 8, column, 0)
    for n in range(8):
        inner(n).wait()
        edge(n, 0).wait()
        edge(n, 1).wait()


def per_device(frames, attend_gain, wq, wk, wv, wo, mixer_gain, depthwise, mixer_bias):
    hbm = pl.BlockSpec(memory_space=pltpu.HBM)
    vmem = pl.BlockSpec(memory_space=pltpu.VMEM)
    dma = pltpu.SemaphoreType.DMA
    bias = mixer_bias.reshape(1, D)
    padded, mixed = pl.pallas_call(
        kernel,
        out_shape=(
            jax.ShapeDtypeStruct((8, ROWS + 2 * EDGE, 128), F32),
            jax.ShapeDtypeStruct((8, ROWS, 128), F32),
        ),
        in_specs=[hbm] * 9,
        out_specs=(vmem, vmem),
        scratch_shapes=[
            pltpu.VMEM((ROWS, D), F32),
            pltpu.VMEM((1, D), F32),
            *[pltpu.VMEM((D, D), BF16)] * 4,
            pltpu.VMEM((1, D), F32),
            pltpu.VMEM((ROWS, D), BF16),
            pltpu.VMEM((HEADS, HALF, 128), BF16),
            pltpu.VMEM((HEADS, ROWS, 128), BF16),
            pltpu.VMEM((CHIPS, HALF, 128), BF16),
            pltpu.VMEM((CHIPS * 2 * ROWS, 128), BF16),
            pltpu.VMEM((CHIPS * ROWS, 128), BF16),
            pltpu.VMEM((CHIPS * 2 * ROWS, 128), BF16),
            pltpu.VMEM((CHIPS * ROWS, 128), F32),
            pltpu.VMEM((CHIPS * ROWS, 128), F32),
            pltpu.VMEM((CHIPS, HALF, 128), BF16),
            pltpu.VMEM((HEADS, HALF, 128), BF16),
            pltpu.VMEM((ROWS, D), BF16),
            pltpu.VMEM((2, 8, EDGE, 128), F32),
            pltpu.VMEM((2, 8, EDGE, 128), F32),
            pltpu.VMEM((KERNEL, D), F32),
            pltpu.VMEM((1, D), F32),
            dma((9,)), dma((3,)),
            *[dma((CHIPS,))] * 8,
            dma((2,)), dma((2,)),
        ],
        compiler_params=pltpu.CompilerParams(
            collective_id=0, has_side_effects=True, vmem_limit_bytes=GRANT
        ),
        name="block",
    )(
        *(
            pltpu.with_memory_space_constraint(value, pltpu.HBM)
            for value in (
                frames, attend_gain.reshape(1, D), wq, wk, wv, wo, mixer_gain.reshape(1, D), depthwise, bias,
            )
        )
    )
    return pl.pallas_call(
        convolve,
        out_shape=jax.ShapeDtypeStruct((ROWS, D), F32),
        in_specs=[vmem] * 4,
        out_specs=hbm,
        scratch_shapes=[pltpu.VMEM((8, 2, EDGE, 128), F32), dma((8,)), dma((8, 2))],
        compiler_params=pltpu.CompilerParams(vmem_limit_bytes=16 * 1024 * 1024),
        name="convolve",
    )(padded, mixed, depthwise, bias)


def solution(mesh):
    in_specs = (P(("session", "ctx"), None), P(), P(), P(), P(), P(), P(), P(), P())
    return jax.shard_map(
        per_device, mesh=mesh, in_specs=in_specs, out_specs=P(("session", "ctx"), None), check_vma=False
    )
```

```python
import functools
import math

import jax
import jax.numpy as jnp
from jax import lax
from jax.experimental import pallas as pl
from jax.experimental.pallas import tpu as pltpu
from jax.sharding import PartitionSpec as P

F32, BF16 = jnp.float32, jnp.bfloat16
MESH = pl.DeviceIdType.MESH
HEADS = 16
HEAD = 64
KERNEL = 31
ROWS = 192
HALF = ROWS // 2
D = 1024
CHIPS = 16
EDGE = 16
BQ = 4 * ROWS
GRANT = 48 * 1024 * 1024
BK = 8 * ROWS
SCALE = HEAD**-0.5 * math.log2(math.e)
OFFSETS = (
    (0, 0), (0, 1), (0, 7), (1, 0),
    (0, 2), (0, 6), (1, 1), (1, 7),
    (0, 3), (0, 5), (1, 2), (1, 6),
    (0, 4), (1, 3), (1, 5), (1, 4),
)


STEPS = (
    ((0, 0), (1, 0)), ((0, 1), (1, 1)), ((2, 0), (2, 1)), ((3, 0), (3, 1)),
    ((3, 2), (2, 2)), ((3, 3), (2, 3)), ((1, 2), (1, 3)), ((0, 2), (0, 3)),
)


def pick(step, table):
    value = jnp.int32(table[0])
    for n in range(1, len(table)):
        if table[n] != table[0]:
            value = jnp.where(step == n, table[n], value)
    return value


def rows_at(index, size):
    return pl.ds(pl.multiple_of(index * size, size), size)


def norm(values, gain):
    center = jnp.mean(values, axis=1, keepdims=True)
    spread = jnp.mean(jnp.square(values - center), axis=1, keepdims=True)
    return (values - center) * lax.rsqrt(spread + 1e-05) * gain


def low_lanes(shape):
    return lax.broadcasted_iota(jnp.int32, shape, 1) < HEAD


def swap(values):
    return pltpu.roll(values, HEAD, 1)


def mix(n, starts, padded, attended, taps_ref, bias_ref, out, shift):
    lanes = rows_at(n, 128)
    taps = taps_ref[:, lanes]
    bias = jnp.broadcast_to(bias_ref[:, lanes], (8, 128))
    for at in starts:
        total = bias
        for tap in range(KERNEL):
            total = total + padded[n, at + tap + 1 : at + tap + 9, :] * taps[tap : tap + 1, :]
        out[n, at - shift : at - shift + 8, :] = attended[n, at : at + 8, :] + total / (1.0 + jnp.exp(-total))


def kernel(
    frames_hbm, again_hbm, wq_hbm, wk_hbm, wv_hbm, wo_hbm, mgain_hbm, taps_hbm, bias_hbm,
    padded, mixed,
    frames, again_ref, wq, wk, wv, wo, mgain_ref, normed,
    sendq, sendkv, qbuf, kvbuf, qx, vx, m_ref, o_ref, sendc, cbuf, context, edges, halos, taps_ref, bias_ref,
    load_sem, own_sem, q_send, q_recv, kv_send, kv_recv, f_send, f_recv, c_send, c_recv, h_send, h_recv,
):
    ctx = lax.axis_index("ctx")
    core = lax.rem(ctx, 2)
    chip = ctx // 2
    z, xh = lax.rem(chip, 8), chip // 8
    partner = chip * 2 + 1 - core

    def toward(r):
        dx, dz = OFFSETS[r]
        return lax.rem(xh + dx, 2) * 8 + lax.rem(z + dz, 8)

    def behind(r):
        dx, dz = OFFSETS[r]
        return lax.rem(xh + dx, 2) * 8 + lax.rem(z + 8 - dz, 8)

    def remote(src, dst, send, recv, target):
        return pltpu.make_async_remote_copy(
            src_ref=src, dst_ref=dst, send_sem=send, recv_sem=recv, device_id={"ctx": target}, device_id_type=MESH
        )
    pieces = [slice(g * 256, g * 256 + 256) for g in range(4)]
    loads = [
        pltpu.make_async_copy(src, dst, load_sem.at[n])
        for n, (src, dst) in enumerate(
            (
                (frames_hbm, frames), (again_hbm, again_ref),
                *[(wq_hbm.at[:, piece], wq.at[:, piece]) for piece in pieces],
                (wk_hbm, wk), (wv_hbm, wv),
                (wo_hbm, wo), (mgain_hbm, mgain_ref), (taps_hbm, taps_ref), (bias_hbm, bias_ref),
            )
        )
    ]
    for load in loads:
        load.start()

    barrier = pltpu.get_barrier_semaphore()
    greeted = [toward(r) * 2 + core for r in range(1, CHIPS)]
    greeted += [partner, lax.rem(ctx + 31 + 2 * core, 32)]
    for device in greeted:
        pl.semaphore_signal(barrier, inc=1, device_id={"ctx": device}, device_id_type=MESH)

    loads[0].wait()
    loads[1].wait()
    normed[...] = norm(frames[...], again_ref[...]).astype(BF16)
    low = low_lanes((ROWS, 128))
    low_half = low_lanes((HALF, 128))
    for g in range(4):
        loads[2 + g].wait()
        q = jnp.dot(normed[...], wq[:, g * 256 : g * 256 + 256], preferred_element_type=F32)
        for pair in range(2):
            piece = q[:, pair * 128 : pair * 128 + 128]
            top, bottom = piece[:HALF], piece[HALF:]
            sendq[4 * g + 2 * pair] = jnp.where(low_half, top, swap(bottom)).astype(BF16)
            sendq[4 * g + 2 * pair + 1] = jnp.where(low_half, swap(top), bottom).astype(BF16)

    def q_copy(r):
        p = toward(r)
        return remote(sendq.at[p], qbuf.at[r], q_send.at[r], q_recv.at[r], p * 2 + core)

    def kv_rows(slot, which):
        return pl.ds(pl.multiple_of((slot * 2 + which) * ROWS, ROWS), ROWS)

    def kv_copy(r):
        p = toward(r)
        return remote(sendkv.at[p], kvbuf.at[kv_rows(r, core)], kv_send.at[r], kv_recv.at[r], p * 2 + core)

    q_copies, kv_copies = [None] * CHIPS, [None] * CHIPS

    def send(order):
        for kind, r in order:
            copy = q_copy(r) if kind == "q" else kv_copy(r)
            copy.start()
            (q_copies if kind == "q" else kv_copies)[r] = copy

    own_q = pltpu.make_async_copy(sendq.at[chip], qbuf.at[0], own_sem.at[0])
    own_q.start()
    loads[6].wait()
    loads[7].wait()
    for g in range(4):
        k = jnp.dot(normed[...], wk[:, g * 256 : g * 256 + 256], preferred_element_type=F32)
        v = jnp.dot(normed[...], wv[:, g * 256 : g * 256 + 256], preferred_element_type=F32)
        for pair in range(2):
            kp, vp = k[:, pair * 128 : pair * 128 + 128], v[:, pair * 128 : pair * 128 + 128]
            sendkv[4 * g + 2 * pair] = jnp.where(low, kp, swap(vp)).astype(BF16)
            sendkv[4 * g + 2 * pair + 1] = jnp.where(low, swap(kp), vp).astype(BF16)
    def reset(n, carry):
        m_ref[rows_at(n, BQ), :] = jnp.full((BQ, 128), -jnp.inf, F32)
        o_ref[rows_at(n, BQ), :] = jnp.zeros((BQ, 128), F32)
        return carry

    lax.fori_loop(0, CHIPS * ROWS // BQ, reset, 0)
    pl.semaphore_wait(barrier, len(greeted))
    send([("q", r) for r in range(1, 8)])
    own_kv = pltpu.make_async_copy(sendkv.at[chip], kvbuf.at[kv_rows(0, core)], own_sem.at[1])
    own_forward = remote(sendkv.at[chip], kvbuf.at[kv_rows(0, core)], f_send.at[0], f_recv.at[0], partner)
    own_kv.start()
    own_forward.start()
    send([("kv", r) for r in range(1, 8)] + [("q", r) for r in range(8, CHIPS)] + [("kv", r) for r in range(8, CHIPS)])

    def q_arrival(slot):
        return remote(sendq.at[0], qbuf.at[slot], q_send.at[slot], q_recv.at[slot], partner)

    def kv_arrival(slot):
        return remote(sendkv.at[0], kvbuf.at[kv_rows(slot, core)], kv_send.at[slot], kv_recv.at[slot], partner)

    def forward(slot):
        mine = kvbuf.at[kv_rows(slot, core)]
        return remote(mine, mine, f_send.at[slot], f_recv.at[slot], partner)

    def forwarded(slot):
        theirs = kvbuf.at[kv_rows(slot, 1 - core)]
        return remote(theirs, theirs, f_send.at[slot], f_recv.at[slot], partner)
    own_q.wait()
    own_kv.wait()
    for r in range(1, 4):
        kv_arrival(r).wait_recv()
        forward(r).start()

    def unpack_q(block, skip=0):
        for s in range(skip, 4):
            q_arrival(block * 4 + s).wait_recv()
        for s in range(4):
            x = qbuf[block * 4 + s].astype(F32)
            at = pl.multiple_of((block * 4 + s) * ROWS, ROWS)
            qx[pl.ds(at, HALF), :] = jnp.where(low_half, x, 0.0).astype(BF16)
            qx[pl.ds(at + HALF, HALF), :] = jnp.where(low_half, swap(x), 0.0).astype(BF16)

    def pass_on(chunk):
        for s in range(4):
            kv_arrival(chunk * 4 + s).wait_recv()
            forward(chunk * 4 + s).start()

    low_wide = low_lanes((8 * ROWS, 128))

    def open_chunk(chunk):
        for s in range(4):
            forwarded(chunk * 4 + s).wait_recv()
        at = rows_at(chunk, BK)
        x = kvbuf[at, :]
        vx[at, :] = jnp.where(low_wide, jnp.ones_like(x), x)

    def attend(i, j):
        q = qx[rows_at(i, BQ), :]
        scores = lax.dot_general(
            q, kvbuf[rows_at(j, BK), :], (((1,), (1,)), ((), ())), preferred_element_type=F32
        )
        old = m_ref[rows_at(i, BQ), :]
        new = jnp.maximum(old, jnp.max(scores, axis=1, keepdims=True))
        weights = jnp.exp2((scores - jnp.concatenate([new] * (BK // 128), axis=1)) * SCALE).astype(BF16)
        part = jnp.dot(weights, vx[rows_at(j, BK), :], preferred_element_type=F32)
        o_ref[rows_at(i, BQ), :] = o_ref[rows_at(i, BQ), :] * jnp.exp2((old - new) * SCALE) + part
        m_ref[rows_at(i, BQ), :] = new

    def give_back(block):
        for s in range(4):
            o = o_ref[(block * 4 + s) * ROWS : (block * 4 + s + 1) * ROWS, :]
            c = o / swap(o)
            sendc[block * 4 + s] = jnp.where(low_half, swap(c[:HALF]), c[HALF:]).astype(BF16)
        for r in range(block * 4, block * 4 + 4):
            if r > 0:
                remote(sendc.at[r], cbuf.at[chip], c_send.at[r], c_recv.at[r], behind(r) * 2 + core).start()
    unpack_q(0, 1)
    unpack_q(1)

    def step(t, carry):
        opened = {0: 0, 1: 1, 4: 2, 5: 3}
        for when, chunk in opened.items():
            @pl.when(t == when)
            def _():
                open_chunk(chunk)
        for when, block in {2: 2, 3: 3}.items():
            @pl.when(t == when)
            def _():
                unpack_q(block)
        for half in range(2):
            attend(pick(t, [pair[half][0] for pair in STEPS]), pick(t, [pair[half][1] for pair in STEPS]))
        for when, chunk in {0: 1, 3: 2, 4: 3}.items():
            @pl.when(t == when)
            def _():
                pass_on(chunk)
        for when, blocks in {5: (3, 2), 6: (1,), 7: (0,)}.items():
            @pl.when(t == when)
            def _():
                for block in blocks:
                    give_back(block)

        return carry
    lax.fori_loop(0, len(STEPS), step, 0)

    own_c = pltpu.make_async_copy(sendc.at[0], cbuf.at[chip], own_sem.at[2])
    own_c.start()
    for load in loads[8:]:
        load.wait()
    own_c.wait()
    for r in range(1, CHIPS):
        remote(sendc.at[r], cbuf.at[toward(r)], c_send.at[r], c_recv.at[r], partner).wait_recv()
    for pair in range(HEADS // 2):
        a, b = cbuf[2 * pair].astype(F32), cbuf[2 * pair + 1].astype(F32)
        cols = slice(pair * 128, pair * 128 + 128)
        context[:HALF, cols] = jnp.where(low_half, a, swap(b)).astype(BF16)
        context[HALF:, cols] = jnp.where(low_half, swap(a), b).astype(BF16)
    total = frames[...] + jnp.dot(context[...], wo[...], preferred_element_type=F32)
    mixer_in = norm(total, mgain_ref[...])
    for n in range(8):
        part = mixer_in[:, n * 128 : n * 128 + 128]
        edges[0, n] = part[:EDGE]
        edges[1, n] = part[ROWS - EDGE :]
        padded[n, EDGE : EDGE + ROWS, :] = part
        mixed[n] = total[:, n * 128 : n * 128 + 128]

    after, before = lax.rem(ctx + 1, 32), lax.rem(ctx + 31, 32)
    up = remote(edges.at[1], halos.at[0], h_send.at[0], h_recv.at[0], after)
    down = remote(edges.at[0], halos.at[1], h_send.at[1], h_recv.at[1], before)
    up.start()
    down.start()

    def interior(n, carry):
        mix(n, range(EDGE, ROWS - EDGE, 8), padded, mixed, taps_ref, bias_ref, mixed, 0)
        return carry

    lax.fori_loop(0, 8, interior, 0)
    up.wait()
    down.wait()
    padded[:, :EDGE, :] = jnp.where(ctx > 0, halos[0], 0.0)
    padded[:, EDGE + ROWS :, :] = jnp.where(ctx < 31, halos[1], 0.0)
    own_forward.wait_send()
    for r in range(1, CHIPS):
        q_copies[r].wait_send()
        kv_copies[r].wait_send()
        forward(r).wait_send()
        remote(sendc.at[r], cbuf.at[chip], c_send.at[r], c_recv.at[r], partner).wait_send()


def convolve(padded_ref, mixed_ref, taps_ref, bias_ref, out_hbm, result, inner_sems, edge_sems):
    def inner(n):
        rows = pl.ds(EDGE, ROWS - 2 * EDGE)
        return pltpu.make_async_copy(mixed_ref.at[n, rows], out_hbm.at[rows, rows_at(n, 128)], inner_sems.at[n])

    def edge(n, side):
        rows = pl.ds(side * (ROWS - EDGE), EDGE)
        return pltpu.make_async_copy(result.at[n, side], out_hbm.at[rows, rows_at(n, 128)], edge_sems.at[n, side])

    for n in range(8):
        inner(n).start()

    def column(n, carry):
        mix(n, range(0, EDGE, 8), padded_ref, mixed_ref, taps_ref, bias_ref, result.at[:, 0], 0)
        mix(n, range(ROWS - EDGE, ROWS, 8), padded_ref, mixed_ref, taps_ref, bias_ref, result.at[:, 1], ROWS - EDGE)
        edge(n, 0).start()
        edge(n, 1).start()
        return carry

    lax.fori_loop(0, 8, column, 0)
    for n in range(8):
        inner(n).wait()
        edge(n, 0).wait()
        edge(n, 1).wait()


def per_device(frames, attend_gain, wq, wk, wv, wo, mixer_gain, depthwise, mixer_bias):
    hbm = pl.BlockSpec(memory_space=pltpu.HBM)
    vmem = pl.BlockSpec(memory_space=pltpu.VMEM)
    dma = pltpu.SemaphoreType.DMA
    bias = mixer_bias.reshape(1, D)
    padded, mixed = pl.pallas_call(
        kernel,
        out_shape=(
            jax.ShapeDtypeStruct((8, ROWS + 2 * EDGE, 128), F32),
            jax.ShapeDtypeStruct((8, ROWS, 128), F32),
        ),
        in_specs=[hbm] * 9,
        out_specs=(vmem, vmem),
        scratch_shapes=[
            pltpu.VMEM((ROWS, D), F32),
            pltpu.VMEM((1, D), F32),
            *[pltpu.VMEM((D, D), BF16)] * 4,
            pltpu.VMEM((1, D), F32),
            pltpu.VMEM((ROWS, D), BF16),
            pltpu.VMEM((HEADS, HALF, 128), BF16),
            pltpu.VMEM((HEADS, ROWS, 128), BF16),
            pltpu.VMEM((CHIPS, HALF, 128), BF16),
            pltpu.VMEM((CHIPS * 2 * ROWS, 128), BF16),
            pltpu.VMEM((CHIPS * ROWS, 128), BF16),
            pltpu.VMEM((CHIPS * 2 * ROWS, 128), BF16),
            pltpu.VMEM((CHIPS * ROWS, 128), F32),
            pltpu.VMEM((CHIPS * ROWS, 128), F32),
            pltpu.VMEM((CHIPS, HALF, 128), BF16),
            pltpu.VMEM((HEADS, HALF, 128), BF16),
            pltpu.VMEM((ROWS, D), BF16),
            pltpu.VMEM((2, 8, EDGE, 128), F32),
            pltpu.VMEM((2, 8, EDGE, 128), F32),
            pltpu.VMEM((KERNEL, D), F32),
            pltpu.VMEM((1, D), F32),
            dma((12,)), dma((3,)),
            *[dma((CHIPS,))] * 8,
            dma((2,)), dma((2,)),
        ],
        compiler_params=pltpu.CompilerParams(
            collective_id=0, has_side_effects=True, vmem_limit_bytes=GRANT
        ),
        name="block",
    )(
        *(
            pltpu.with_memory_space_constraint(value, pltpu.HBM)
            for value in (
                frames, attend_gain.reshape(1, D), wq, wk, wv, wo, mixer_gain.reshape(1, D), depthwise, bias,
            )
        )
    )
    return pl.pallas_call(
        convolve,
        out_shape=jax.ShapeDtypeStruct((ROWS, D), F32),
        in_specs=[vmem] * 4,
        out_specs=hbm,
        scratch_shapes=[pltpu.VMEM((8, 2, EDGE, 128), F32), dma((8,)), dma((8, 2))],
        compiler_params=pltpu.CompilerParams(vmem_limit_bytes=16 * 1024 * 1024),
        name="convolve",
    )(padded, mixed, depthwise, bias)


def solution(mesh):
    in_specs = (P(("session", "ctx"), None), P(), P(), P(), P(), P(), P(), P(), P())
    return jax.shard_map(
        per_device, mesh=mesh, in_specs=in_specs, out_specs=P(("session", "ctx"), None), check_vma=False
    )
```

```python
import functools
import math

import jax
import jax.numpy as jnp
from jax import lax
from jax.experimental import pallas as pl
from jax.experimental.pallas import tpu as pltpu
from jax.sharding import PartitionSpec as P

F32, BF16 = jnp.float32, jnp.bfloat16
MESH = pl.DeviceIdType.MESH
HEADS = 16
HEAD = 64
KERNEL = 31
ROWS = 192
HALF = ROWS // 2
D = 1024
CHIPS = 16
EDGE = 16
BQ = 4 * ROWS
GRANT = 48 * 1024 * 1024
BK = 8 * ROWS
SCALE = HEAD**-0.5 * math.log2(math.e)
OFFSETS = (
    (0, 0), (0, 1), (0, 7), (1, 0),
    (0, 2), (0, 6), (1, 1), (1, 7),
    (0, 3), (0, 5), (1, 2), (1, 6),
    (0, 4), (1, 3), (1, 5), (1, 4),
)


STEPS = (((0, 0), (1, 0)), ((0, 1), (1, 1)), ((2, 0), (2, 1)), ((3, 0), (3, 1)), ((3, 2), (2, 2)))


def pick(step, table):
    value = jnp.int32(table[0])
    for n in range(1, len(table)):
        if table[n] != table[0]:
            value = jnp.where(step == n, table[n], value)
    return value


def rows_at(index, size):
    if isinstance(index, int):
        return pl.ds(index * size, size)
    return pl.ds(pl.multiple_of(index * size, size), size)


def norm(values, gain):
    center = jnp.mean(values, axis=1, keepdims=True)
    spread = jnp.mean(jnp.square(values - center), axis=1, keepdims=True)
    return (values - center) * lax.rsqrt(spread + 1e-05) * gain


def low_lanes(shape):
    return lax.broadcasted_iota(jnp.int32, shape, 1) < HEAD


def swap(values):
    return pltpu.roll(values, HEAD, 1)


def mix(n, starts, padded, attended, taps_ref, bias_ref, out, shift):
    lanes = rows_at(n, 128)
    taps = taps_ref[:, lanes]
    bias = jnp.broadcast_to(bias_ref[:, lanes], (8, 128))
    for at in starts:
        total = bias
        for tap in range(KERNEL):
            total = total + padded[n, at + tap + 1 : at + tap + 9, :] * taps[tap : tap + 1, :]
        out[n, at - shift : at - shift + 8, :] = attended[n, at : at + 8, :] + total / (1.0 + jnp.exp(-total))


def kernel(
    frames_hbm, again_hbm, wq_hbm, wk_hbm, wv_hbm, wo_hbm, mgain_hbm, taps_hbm, bias_hbm,
    padded, mixed,
    frames, again_ref, wq, wk, wv, wo, mgain_ref, normed,
    sendq, sendkv, qbuf, kvbuf, qx, vx, m_ref, o_ref, sendc, cbuf, context, edges, halos, taps_ref, bias_ref,
    load_sem, own_sem, q_send, q_recv, kv_send, kv_recv, f_send, f_recv, c_send, c_recv, h_send, h_recv,
):
    ctx = lax.axis_index("ctx")
    core = lax.rem(ctx, 2)
    chip = ctx // 2
    z, xh = lax.rem(chip, 8), chip // 8
    partner = chip * 2 + 1 - core

    def toward(r):
        dx, dz = OFFSETS[r]
        return lax.rem(xh + dx, 2) * 8 + lax.rem(z + dz, 8)

    def behind(r):
        dx, dz = OFFSETS[r]
        return lax.rem(xh + dx, 2) * 8 + lax.rem(z + 8 - dz, 8)

    def remote(src, dst, send, recv, target):
        return pltpu.make_async_remote_copy(
            src_ref=src, dst_ref=dst, send_sem=send, recv_sem=recv, device_id={"ctx": target}, device_id_type=MESH
        )
    loads = [
        pltpu.make_async_copy(src, dst, load_sem.at[n])
        for n, (src, dst) in enumerate(
            (
                (frames_hbm, frames), (again_hbm, again_ref),
                (wq_hbm, wq), (wk_hbm, wk), (wv_hbm, wv),
                (wo_hbm, wo), (mgain_hbm, mgain_ref), (taps_hbm, taps_ref), (bias_hbm, bias_ref),
            )
        )
    ]
    for load in loads[:3]:
        load.start()

    barrier = pltpu.get_barrier_semaphore()
    greeted = [toward(r) * 2 + core for r in range(1, CHIPS)]
    greeted += [partner, lax.rem(ctx + 31 + 2 * core, 32)]
    for device in greeted:
        pl.semaphore_signal(barrier, inc=1, device_id={"ctx": device}, device_id_type=MESH)

    loads[0].wait()
    loads[1].wait()
    for load in loads[3:5]:
        load.start()
    normed[...] = norm(frames[...], again_ref[...]).astype(BF16)
    low = low_lanes((ROWS, 128))
    low_half = low_lanes((HALF, 128))
    loads[2].wait()
    for g in range(4):
        q = jnp.dot(normed[...], wq[:, g * 256 : g * 256 + 256], preferred_element_type=F32)
        for pair in range(2):
            piece = q[:, pair * 128 : pair * 128 + 128]
            top, bottom = piece[:HALF], piece[HALF:]
            sendq[4 * g + 2 * pair] = jnp.where(low_half, top, swap(bottom)).astype(BF16)
            sendq[4 * g + 2 * pair + 1] = jnp.where(low_half, swap(top), bottom).astype(BF16)

    def q_copy(r):
        p = toward(r)
        return remote(sendq.at[p], qbuf.at[r], q_send.at[r], q_recv.at[r], p * 2 + core)

    def kv_rows(slot, which):
        return pl.ds(pl.multiple_of((slot * 2 + which) * ROWS, ROWS), ROWS)

    def kv_copy(r):
        p = toward(r)
        return remote(sendkv.at[p], kvbuf.at[kv_rows(r, core)], kv_send.at[r], kv_recv.at[r], p * 2 + core)

    q_copies, kv_copies = [None] * CHIPS, [None] * CHIPS

    def send(order):
        for kind, r in order:
            copy = q_copy(r) if kind == "q" else kv_copy(r)
            copy.start()
            (q_copies if kind == "q" else kv_copies)[r] = copy

    own_q = pltpu.make_async_copy(sendq.at[chip], qbuf.at[0], own_sem.at[0])
    own_q.start()
    pl.semaphore_wait(barrier, len(greeted))
    send([("q", r) for r in range(1, 8)])
    for load in loads[5:]:
        load.start()
    loads[3].wait()
    loads[4].wait()
    for g in range(4):
        k = jnp.dot(normed[...], wk[:, g * 256 : g * 256 + 256], preferred_element_type=F32)
        v = jnp.dot(normed[...], wv[:, g * 256 : g * 256 + 256], preferred_element_type=F32)
        for pair in range(2):
            kp, vp = k[:, pair * 128 : pair * 128 + 128], v[:, pair * 128 : pair * 128 + 128]
            sendkv[4 * g + 2 * pair] = jnp.where(low, kp, swap(vp)).astype(BF16)
            sendkv[4 * g + 2 * pair + 1] = jnp.where(low, swap(kp), vp).astype(BF16)
    own_kv = pltpu.make_async_copy(sendkv.at[chip], kvbuf.at[kv_rows(0, core)], own_sem.at[1])
    own_forward = remote(sendkv.at[chip], kvbuf.at[kv_rows(0, core)], f_send.at[0], f_recv.at[0], partner)
    own_kv.start()
    own_forward.start()
    send([("kv", r) for r in range(1, 8)] + [("q", r) for r in range(8, CHIPS)] + [("kv", r) for r in range(8, CHIPS)])

    def q_arrival(slot):
        return remote(sendq.at[0], qbuf.at[slot], q_send.at[slot], q_recv.at[slot], partner)

    def kv_arrival(slot):
        return remote(sendkv.at[0], kvbuf.at[kv_rows(slot, core)], kv_send.at[slot], kv_recv.at[slot], partner)

    def forward(slot):
        mine = kvbuf.at[kv_rows(slot, core)]
        return remote(mine, mine, f_send.at[slot], f_recv.at[slot], partner)

    def forwarded(slot):
        theirs = kvbuf.at[kv_rows(slot, 1 - core)]
        return remote(theirs, theirs, f_send.at[slot], f_recv.at[slot], partner)

    def reset(n, carry):
        m_ref[rows_at(n, BQ), :] = jnp.full((BQ, 128), -jnp.inf, F32)
        o_ref[rows_at(n, BQ), :] = jnp.zeros((BQ, 128), F32)
        return carry

    lax.fori_loop(0, CHIPS * ROWS // BQ, reset, 0)
    own_q.wait()
    own_kv.wait()
    for r in range(1, 4):
        kv_arrival(r).wait_recv()
        forward(r).start()

    def unpack_q(block, skip=0):
        for s in range(skip, 4):
            q_arrival(block * 4 + s).wait_recv()
        for s in range(4):
            x = qbuf[block * 4 + s].astype(F32)
            at = pl.multiple_of((block * 4 + s) * ROWS, ROWS)
            qx[pl.ds(at, HALF), :] = jnp.where(low_half, x, 0.0).astype(BF16)
            qx[pl.ds(at + HALF, HALF), :] = jnp.where(low_half, swap(x), 0.0).astype(BF16)

    def pass_on(chunk):
        for s in range(4):
            kv_arrival(chunk * 4 + s).wait_recv()
            forward(chunk * 4 + s).start()

    low_wide = low_lanes((8 * ROWS, 128))

    def open_chunk(chunk):
        for s in range(4):
            forwarded(chunk * 4 + s).wait_recv()
        at = rows_at(chunk, BK)
        x = kvbuf[at, :]
        vx[at, :] = jnp.where(low_wide, jnp.ones_like(x), x)

    def attend(i, j):
        q = qx[rows_at(i, BQ), :]
        scores = lax.dot_general(
            q, kvbuf[rows_at(j, BK), :], (((1,), (1,)), ((), ())), preferred_element_type=F32
        )
        old = m_ref[rows_at(i, BQ), :]
        new = jnp.maximum(old, jnp.max(scores, axis=1, keepdims=True))
        weights = jnp.exp2((scores - jnp.concatenate([new] * (BK // 128), axis=1)) * SCALE).astype(BF16)
        part = jnp.dot(weights, vx[rows_at(j, BK), :], preferred_element_type=F32)
        o_ref[rows_at(i, BQ), :] = o_ref[rows_at(i, BQ), :] * jnp.exp2((old - new) * SCALE) + part
        m_ref[rows_at(i, BQ), :] = new

    def give_back(block):
        for s in range(4):
            o = o_ref[(block * 4 + s) * ROWS : (block * 4 + s + 1) * ROWS, :]
            c = o / swap(o)
            sendc[block * 4 + s] = jnp.where(low_half, swap(c[:HALF]), c[HALF:]).astype(BF16)
        for r in range(block * 4, block * 4 + 4):
            if r > 0:
                remote(sendc.at[r], cbuf.at[chip], c_send.at[r], c_recv.at[r], behind(r) * 2 + core).start()
    unpack_q(0, 1)
    unpack_q(1)

    def step(t, carry):
        opened = {0: 0, 1: 1, 4: 2}
        for when, chunk in opened.items():
            @pl.when(t == when)
            def _():
                open_chunk(chunk)
        for when, block in {2: 2, 3: 3}.items():
            @pl.when(t == when)
            def _():
                unpack_q(block)
        for half in range(2):
            attend(pick(t, [pair[half][0] for pair in STEPS]), pick(t, [pair[half][1] for pair in STEPS]))
        for when, chunk in {0: 1, 3: 2, 4: 3}.items():
            @pl.when(t == when)
            def _():
                pass_on(chunk)

        return carry
    lax.fori_loop(0, len(STEPS), step, 0)
    attend(1, 2)
    open_chunk(3)
    attend(3, 3)
    give_back(3)
    attend(2, 3)
    attend(1, 3)
    give_back(2)
    give_back(1)
    attend(0, 2)
    attend(0, 3)
    give_back(0)

    own_c = pltpu.make_async_copy(sendc.at[0], cbuf.at[chip], own_sem.at[2])
    own_c.start()
    for load in loads[5:]:
        load.wait()
    own_c.wait()
    for r in range(1, CHIPS):
        remote(sendc.at[r], cbuf.at[toward(r)], c_send.at[r], c_recv.at[r], partner).wait_recv()
    for pair in range(HEADS // 2):
        a, b = cbuf[2 * pair].astype(F32), cbuf[2 * pair + 1].astype(F32)
        cols = slice(pair * 128, pair * 128 + 128)
        context[:HALF, cols] = jnp.where(low_half, a, swap(b)).astype(BF16)
        context[HALF:, cols] = jnp.where(low_half, swap(a), b).astype(BF16)
    total = frames[...] + jnp.dot(context[...], wo[...], preferred_element_type=F32)
    mixer_in = norm(total, mgain_ref[...])
    for n in range(8):
        part = mixer_in[:, n * 128 : n * 128 + 128]
        edges[0, n] = part[:EDGE]
        edges[1, n] = part[ROWS - EDGE :]
        padded[n, EDGE : EDGE + ROWS, :] = part
        mixed[n] = total[:, n * 128 : n * 128 + 128]

    after, before = lax.rem(ctx + 1, 32), lax.rem(ctx + 31, 32)
    up = remote(edges.at[1], halos.at[0], h_send.at[0], h_recv.at[0], after)
    down = remote(edges.at[0], halos.at[1], h_send.at[1], h_recv.at[1], before)
    up.start()
    down.start()

    def interior(n, carry):
        mix(n, range(EDGE, ROWS - EDGE, 8), padded, mixed, taps_ref, bias_ref, mixed, 0)
        return carry

    lax.fori_loop(0, 8, interior, 0)
    up.wait()
    down.wait()
    padded[:, :EDGE, :] = jnp.where(ctx > 0, halos[0], 0.0)
    padded[:, EDGE + ROWS :, :] = jnp.where(ctx < 31, halos[1], 0.0)
    own_forward.wait_send()
    for r in range(1, CHIPS):
        q_copies[r].wait_send()
        kv_copies[r].wait_send()
        forward(r).wait_send()
        remote(sendc.at[r], cbuf.at[chip], c_send.at[r], c_recv.at[r], partner).wait_send()


def convolve(padded_ref, mixed_ref, taps_ref, bias_ref, out_hbm, result, inner_sems, edge_sems):
    def inner(n):
        rows = pl.ds(EDGE, ROWS - 2 * EDGE)
        return pltpu.make_async_copy(mixed_ref.at[n, rows], out_hbm.at[rows, rows_at(n, 128)], inner_sems.at[n])

    def edge(n, side):
        rows = pl.ds(side * (ROWS - EDGE), EDGE)
        return pltpu.make_async_copy(result.at[n, side], out_hbm.at[rows, rows_at(n, 128)], edge_sems.at[n, side])

    for n in range(8):
        inner(n).start()

    def column(n, carry):
        mix(n, range(0, EDGE, 8), padded_ref, mixed_ref, taps_ref, bias_ref, result.at[:, 0], 0)
        mix(n, range(ROWS - EDGE, ROWS, 8), padded_ref, mixed_ref, taps_ref, bias_ref, result.at[:, 1], ROWS - EDGE)
        edge(n, 0).start()
        edge(n, 1).start()
        return carry

    lax.fori_loop(0, 8, column, 0)
    for n in range(8):
        inner(n).wait()
        edge(n, 0).wait()
        edge(n, 1).wait()


def per_device(frames, attend_gain, wq, wk, wv, wo, mixer_gain, depthwise, mixer_bias):
    hbm = pl.BlockSpec(memory_space=pltpu.HBM)
    vmem = pl.BlockSpec(memory_space=pltpu.VMEM)
    dma = pltpu.SemaphoreType.DMA
    bias = mixer_bias.reshape(1, D)
    padded, mixed = pl.pallas_call(
        kernel,
        out_shape=(
            jax.ShapeDtypeStruct((8, ROWS + 2 * EDGE, 128), F32),
            jax.ShapeDtypeStruct((8, ROWS, 128), F32),
        ),
        in_specs=[hbm] * 9,
        out_specs=(vmem, vmem),
        scratch_shapes=[
            pltpu.VMEM((ROWS, D), F32),
            pltpu.VMEM((1, D), F32),
            *[pltpu.VMEM((D, D), BF16)] * 4,
            pltpu.VMEM((1, D), F32),
            pltpu.VMEM((ROWS, D), BF16),
            pltpu.VMEM((HEADS, HALF, 128), BF16),
            pltpu.VMEM((HEADS, ROWS, 128), BF16),
            pltpu.VMEM((CHIPS, HALF, 128), BF16),
            pltpu.VMEM((CHIPS * 2 * ROWS, 128), BF16),
            pltpu.VMEM((CHIPS * ROWS, 128), BF16),
            pltpu.VMEM((CHIPS * 2 * ROWS, 128), BF16),
            pltpu.VMEM((CHIPS * ROWS, 128), F32),
            pltpu.VMEM((CHIPS * ROWS, 128), F32),
            pltpu.VMEM((CHIPS, HALF, 128), BF16),
            pltpu.VMEM((HEADS, HALF, 128), BF16),
            pltpu.VMEM((ROWS, D), BF16),
            pltpu.VMEM((2, 8, EDGE, 128), F32),
            pltpu.VMEM((2, 8, EDGE, 128), F32),
            pltpu.VMEM((KERNEL, D), F32),
            pltpu.VMEM((1, D), F32),
            dma((9,)), dma((3,)),
            *[dma((CHIPS,))] * 8,
            dma((2,)), dma((2,)),
        ],
        compiler_params=pltpu.CompilerParams(
            collective_id=0, has_side_effects=True, vmem_limit_bytes=GRANT
        ),
        name="block",
    )(
        *(
            pltpu.with_memory_space_constraint(value, pltpu.HBM)
            for value in (
                frames, attend_gain.reshape(1, D), wq, wk, wv, wo, mixer_gain.reshape(1, D), depthwise, bias,
            )
        )
    )
    return pl.pallas_call(
        convolve,
        out_shape=jax.ShapeDtypeStruct((ROWS, D), F32),
        in_specs=[vmem] * 4,
        out_specs=hbm,
        scratch_shapes=[pltpu.VMEM((8, 2, EDGE, 128), F32), dma((8,)), dma((8, 2))],
        compiler_params=pltpu.CompilerParams(vmem_limit_bytes=16 * 1024 * 1024),
        name="convolve",
    )(padded, mixed, depthwise, bias)


def solution(mesh):
    in_specs = (P(("session", "ctx"), None), P(), P(), P(), P(), P(), P(), P(), P())
    return jax.shard_map(
        per_device, mesh=mesh, in_specs=in_specs, out_specs=P(("session", "ctx"), None), check_vma=False
    )
```

```python
import functools
import math

import jax
import jax.numpy as jnp
from jax import lax
from jax.experimental import pallas as pl
from jax.experimental.pallas import tpu as pltpu
from jax.sharding import PartitionSpec as P

F32, BF16 = jnp.float32, jnp.bfloat16
MESH = pl.DeviceIdType.MESH
HEADS = 16
HEAD = 64
KERNEL = 31
ROWS = 192
HALF = ROWS // 2
D = 1024
CHIPS = 16
EDGE = 16
BQ = 4 * ROWS
GRANT = 48 * 1024 * 1024
BK = 8 * ROWS
SCALE = HEAD**-0.5 * math.log2(math.e)
OFFSETS = (
    (0, 0), (0, 1), (0, 7), (1, 0),
    (0, 2), (0, 6), (1, 1), (1, 7),
    (0, 3), (0, 5), (1, 2), (1, 6),
    (0, 4), (1, 3), (1, 5), (1, 4),
)


STEPS = (((0, 0), (1, 0)), ((0, 1), (1, 1)), ((2, 0), (2, 1)), ((3, 0), (3, 1)), ((3, 2), (2, 2)))


def pick(step, table):
    value = jnp.int32(table[0])
    for n in range(1, len(table)):
        if table[n] != table[0]:
            value = jnp.where(step == n, table[n], value)
    return value


def rows_at(index, size):
    if isinstance(index, int):
        return pl.ds(index * size, size)
    return pl.ds(pl.multiple_of(index * size, size), size)


def norm(values, gain):
    center = jnp.mean(values, axis=1, keepdims=True)
    spread = jnp.mean(jnp.square(values - center), axis=1, keepdims=True)
    return (values - center) * lax.rsqrt(spread + 1e-05) * gain


def low_lanes(shape):
    return lax.broadcasted_iota(jnp.int32, shape, 1) < HEAD


def swap(values):
    return pltpu.roll(values, HEAD, 1)


def mix(n, starts, padded, attended, taps_ref, bias_ref, out, shift):
    lanes = rows_at(n, 128)
    taps = taps_ref[:, lanes]
    bias = jnp.broadcast_to(bias_ref[:, lanes], (8, 128))
    for at in starts:
        total = bias
        for tap in range(KERNEL):
            total = total + padded[n, at + tap + 1 : at + tap + 9, :] * taps[tap : tap + 1, :]
        out[n, at - shift : at - shift + 8, :] = attended[n, at : at + 8, :] + total / (1.0 + jnp.exp(-total))


def kernel(
    frames_hbm, again_hbm, wq_hbm, wk_hbm, wv_hbm, wo_hbm, mgain_hbm, taps_hbm, bias_hbm,
    padded, mixed,
    frames, again_ref, wq, wk, wv, wo, mgain_ref, normed,
    sendq, sendkv, qbuf, kvbuf, qx, vx, m_ref, o_ref, sendc, cbuf, context, edges, halos, taps_ref, bias_ref,
    load_sem, own_sem, q_send, q_recv, kv_send, kv_recv, f_send, f_recv, c_send, c_recv, h_send, h_recv,
):
    ctx = lax.axis_index("ctx")
    core = lax.rem(ctx, 2)
    chip = ctx // 2
    z, xh = lax.rem(chip, 8), chip // 8
    partner = chip * 2 + 1 - core

    def toward(r):
        dx, dz = OFFSETS[r]
        return lax.rem(xh + dx, 2) * 8 + lax.rem(z + dz, 8)

    def behind(r):
        dx, dz = OFFSETS[r]
        return lax.rem(xh + dx, 2) * 8 + lax.rem(z + 8 - dz, 8)

    def remote(src, dst, send, recv, target):
        return pltpu.make_async_remote_copy(
            src_ref=src, dst_ref=dst, send_sem=send, recv_sem=recv, device_id={"ctx": target}, device_id_type=MESH
        )
    loads = [
        pltpu.make_async_copy(src, dst, load_sem.at[n])
        for n, (src, dst) in enumerate(
            (
                (frames_hbm, frames), (again_hbm, again_ref),
                (wq_hbm, wq), (wk_hbm, wk), (wv_hbm, wv),
                (wo_hbm, wo), (mgain_hbm, mgain_ref), (taps_hbm, taps_ref), (bias_hbm, bias_ref),
            )
        )
    ]
    for load in loads[:3]:
        load.start()

    barrier = pltpu.get_barrier_semaphore()
    greeted = [toward(r) * 2 + core for r in range(1, CHIPS)]
    greeted += [partner, lax.rem(ctx + 31 + 2 * core, 32)]
    for device in greeted:
        pl.semaphore_signal(barrier, inc=1, device_id={"ctx": device}, device_id_type=MESH)

    loads[0].wait()
    loads[1].wait()
    for load in loads[3:5]:
        load.start()
    normed[...] = norm(frames[...], again_ref[...]).astype(BF16)
    low = low_lanes((ROWS, 128))
    low_half = low_lanes((HALF, 128))
    loads[2].wait()
    for g in range(4):
        q = jnp.dot(normed[...], wq[:, g * 256 : g * 256 + 256], preferred_element_type=F32)
        for pair in range(2):
            piece = q[:, pair * 128 : pair * 128 + 128]
            top, bottom = piece[:HALF], piece[HALF:]
            sendq[4 * g + 2 * pair] = jnp.where(low_half, top, swap(bottom)).astype(BF16)
            sendq[4 * g + 2 * pair + 1] = jnp.where(low_half, swap(top), bottom).astype(BF16)

    def q_copy(r):
        p = toward(r)
        return remote(sendq.at[p], qbuf.at[r], q_send.at[0], q_recv.at[r // 4], p * 2 + core)

    def kv_rows(slot, which):
        return pl.ds(pl.multiple_of((slot * 2 + which) * ROWS, ROWS), ROWS)

    def kv_copy(r):
        p = toward(r)
        return remote(sendkv.at[p], kvbuf.at[kv_rows(r, core)], kv_send.at[0], kv_recv.at[r // 4], p * 2 + core)

    def send(order):
        for kind, r in order:
            (q_copy(r) if kind == "q" else kv_copy(r)).start()

    own_q = pltpu.make_async_copy(sendq.at[chip], qbuf.at[0], own_sem.at[0])
    own_q.start()
    pl.semaphore_wait(barrier, len(greeted))
    send([("q", r) for r in range(1, 8)])
    for load in loads[5:]:
        load.start()
    loads[3].wait()
    loads[4].wait()
    for g in range(4):
        k = jnp.dot(normed[...], wk[:, g * 256 : g * 256 + 256], preferred_element_type=F32)
        v = jnp.dot(normed[...], wv[:, g * 256 : g * 256 + 256], preferred_element_type=F32)
        for pair in range(2):
            kp, vp = k[:, pair * 128 : pair * 128 + 128], v[:, pair * 128 : pair * 128 + 128]
            sendkv[4 * g + 2 * pair] = jnp.where(low, kp, swap(vp)).astype(BF16)
            sendkv[4 * g + 2 * pair + 1] = jnp.where(low, swap(kp), vp).astype(BF16)
    own_kv = pltpu.make_async_copy(sendkv.at[chip], kvbuf.at[kv_rows(0, core)], own_sem.at[1])
    own_forward = remote(sendkv.at[chip], kvbuf.at[kv_rows(0, core)], f_send.at[0], f_recv.at[0], partner)
    own_kv.start()
    own_forward.start()
    send([("kv", r) for r in range(1, 8)] + [("q", r) for r in range(8, CHIPS)] + [("kv", r) for r in range(8, CHIPS)])

    def await_q(block):
        first = 1 if block == 0 else 0
        group = qbuf.at[pl.ds(block * 4 + first, 4 - first)]
        remote(group, group, q_send.at[0], q_recv.at[block], partner).wait_recv()

    def await_kv(chunk):
        group = kvbuf.at[pl.ds(chunk * BK, (3 if chunk == 0 else 4) * ROWS)]
        remote(group, group, kv_send.at[0], kv_recv.at[chunk], partner).wait_recv()

    def forward(slot):
        mine = kvbuf.at[kv_rows(slot, core)]
        return remote(mine, mine, f_send.at[0], f_recv.at[slot // 4], partner)

    def await_forwarded(chunk):
        group = kvbuf.at[pl.ds(chunk * BK, 4 * ROWS)]
        remote(group, group, f_send.at[0], f_recv.at[chunk], partner).wait_recv()

    def reset(n, carry):
        m_ref[rows_at(n, BQ), :] = jnp.full((BQ, 128), -jnp.inf, F32)
        o_ref[rows_at(n, BQ), :] = jnp.zeros((BQ, 128), F32)
        return carry

    lax.fori_loop(0, CHIPS * ROWS // BQ, reset, 0)
    own_q.wait()
    own_kv.wait()
    await_kv(0)
    for r in range(1, 4):
        forward(r).start()

    def unpack_q(block):
        await_q(block)
        for s in range(4):
            x = qbuf[block * 4 + s].astype(F32)
            at = pl.multiple_of((block * 4 + s) * ROWS, ROWS)
            qx[pl.ds(at, HALF), :] = jnp.where(low_half, x, 0.0).astype(BF16)
            qx[pl.ds(at + HALF, HALF), :] = jnp.where(low_half, swap(x), 0.0).astype(BF16)

    def pass_on(chunk):
        await_kv(chunk)
        for s in range(4):
            forward(chunk * 4 + s).start()

    low_wide = low_lanes((8 * ROWS, 128))

    def open_chunk(chunk):
        await_forwarded(chunk)
        at = rows_at(chunk, BK)
        x = kvbuf[at, :]
        vx[at, :] = jnp.where(low_wide, jnp.ones_like(x), x)

    def attend(i, j):
        q = qx[rows_at(i, BQ), :]
        scores = lax.dot_general(
            q, kvbuf[rows_at(j, BK), :], (((1,), (1,)), ((), ())), preferred_element_type=F32
        )
        old = m_ref[rows_at(i, BQ), :]
        new = jnp.maximum(old, jnp.max(scores, axis=1, keepdims=True))
        weights = jnp.exp2((scores - jnp.concatenate([new] * (BK // 128), axis=1)) * SCALE).astype(BF16)
        part = jnp.dot(weights, vx[rows_at(j, BK), :], preferred_element_type=F32)
        o_ref[rows_at(i, BQ), :] = o_ref[rows_at(i, BQ), :] * jnp.exp2((old - new) * SCALE) + part
        m_ref[rows_at(i, BQ), :] = new

    def give_back(block):
        for s in range(4):
            o = o_ref[(block * 4 + s) * ROWS : (block * 4 + s + 1) * ROWS, :]
            c = o / swap(o)
            sendc[block * 4 + s] = jnp.where(low_half, swap(c[:HALF]), c[HALF:]).astype(BF16)
        for r in range(block * 4, block * 4 + 4):
            if r > 0:
                remote(sendc.at[r], cbuf.at[chip], c_send.at[0], c_recv.at[0], behind(r) * 2 + core).start()
    unpack_q(0)
    unpack_q(1)

    def step(t, carry):
        opened = {0: 0, 1: 1, 4: 2}
        for when, chunk in opened.items():
            @pl.when(t == when)
            def _():
                open_chunk(chunk)
        for when, block in {2: 2, 3: 3}.items():
            @pl.when(t == when)
            def _():
                unpack_q(block)
        for half in range(2):
            attend(pick(t, [pair[half][0] for pair in STEPS]), pick(t, [pair[half][1] for pair in STEPS]))
        for when, chunk in {0: 1, 3: 2, 4: 3}.items():
            @pl.when(t == when)
            def _():
                pass_on(chunk)

        return carry
    lax.fori_loop(0, len(STEPS), step, 0)
    attend(1, 2)
    open_chunk(3)
    attend(3, 3)
    give_back(3)
    attend(2, 3)
    attend(1, 3)
    give_back(2)
    give_back(1)
    attend(0, 2)
    attend(0, 3)
    give_back(0)

    own_c = pltpu.make_async_copy(sendc.at[0], cbuf.at[chip], own_sem.at[2])
    own_c.start()
    for load in loads[5:]:
        load.wait()
    own_c.wait()
    returned = cbuf.at[pl.ds(0, CHIPS - 1)]
    remote(returned, returned, c_send.at[0], c_recv.at[0], partner).wait_recv()
    for pair in range(HEADS // 2):
        a, b = cbuf[2 * pair].astype(F32), cbuf[2 * pair + 1].astype(F32)
        cols = slice(pair * 128, pair * 128 + 128)
        context[:HALF, cols] = jnp.where(low_half, a, swap(b)).astype(BF16)
        context[HALF:, cols] = jnp.where(low_half, swap(a), b).astype(BF16)
    total = frames[...] + jnp.dot(context[...], wo[...], preferred_element_type=F32)
    mixer_in = norm(total, mgain_ref[...])
    for n in range(8):
        part = mixer_in[:, n * 128 : n * 128 + 128]
        edges[0, n] = part[:EDGE]
        edges[1, n] = part[ROWS - EDGE :]
        padded[n, EDGE : EDGE + ROWS, :] = part
        mixed[n] = total[:, n * 128 : n * 128 + 128]

    after, before = lax.rem(ctx + 1, 32), lax.rem(ctx + 31, 32)
    up = remote(edges.at[1], halos.at[0], h_send.at[0], h_recv.at[0], after)
    down = remote(edges.at[0], halos.at[1], h_send.at[1], h_recv.at[1], before)
    up.start()
    down.start()

    def interior(n, carry):
        mix(n, range(EDGE, ROWS - EDGE, 8), padded, mixed, taps_ref, bias_ref, mixed, 0)
        return carry

    lax.fori_loop(0, 8, interior, 0)
    up.wait()
    down.wait()
    padded[:, :EDGE, :] = jnp.where(ctx > 0, halos[0], 0.0)
    padded[:, EDGE + ROWS :, :] = jnp.where(ctx < 31, halos[1], 0.0)
    remote(qbuf.at[pl.ds(0, CHIPS - 1)], qbuf.at[pl.ds(0, CHIPS - 1)], q_send.at[0], q_recv.at[0], partner).wait_send()
    for sem, slots in ((kv_send, CHIPS - 1), (f_send, CHIPS)):
        group = kvbuf.at[pl.ds(0, slots * ROWS)]
        remote(group, group, sem.at[0], kv_recv.at[0], partner).wait_send()
    remote(returned, returned, c_send.at[0], c_recv.at[0], partner).wait_send()


def convolve(padded_ref, mixed_ref, taps_ref, bias_ref, out_hbm, result, sems):
    def inner(n):
        rows = pl.ds(EDGE, ROWS - 2 * EDGE)
        return pltpu.make_async_copy(mixed_ref.at[n, rows], out_hbm.at[rows, rows_at(n, 128)], sems.at[0])

    def edge(n, side):
        rows = pl.ds(side * (ROWS - EDGE), EDGE)
        return pltpu.make_async_copy(result.at[n, side], out_hbm.at[rows, rows_at(n, 128)], sems.at[1])

    for n in range(8):
        inner(n).start()

    def column(n, carry):
        mix(n, range(0, EDGE, 8), padded_ref, mixed_ref, taps_ref, bias_ref, result.at[:, 0], 0)
        mix(n, range(ROWS - EDGE, ROWS, 8), padded_ref, mixed_ref, taps_ref, bias_ref, result.at[:, 1], ROWS - EDGE)
        edge(n, 0).start()
        edge(n, 1).start()
        return carry

    lax.fori_loop(0, 8, column, 0)
    block = mixed_ref.at[:, pl.ds(EDGE, ROWS - 2 * EDGE)]
    pltpu.make_async_copy(block, block, sems.at[0]).wait()
    pltpu.make_async_copy(result, result, sems.at[1]).wait()


def per_device(frames, attend_gain, wq, wk, wv, wo, mixer_gain, depthwise, mixer_bias):
    hbm = pl.BlockSpec(memory_space=pltpu.HBM)
    vmem = pl.BlockSpec(memory_space=pltpu.VMEM)
    dma = pltpu.SemaphoreType.DMA
    bias = mixer_bias.reshape(1, D)
    padded, mixed = pl.pallas_call(
        kernel,
        out_shape=(
            jax.ShapeDtypeStruct((8, ROWS + 2 * EDGE, 128), F32),
            jax.ShapeDtypeStruct((8, ROWS, 128), F32),
        ),
        in_specs=[hbm] * 9,
        out_specs=(vmem, vmem),
        scratch_shapes=[
            pltpu.VMEM((ROWS, D), F32),
            pltpu.VMEM((1, D), F32),
            *[pltpu.VMEM((D, D), BF16)] * 4,
            pltpu.VMEM((1, D), F32),
            pltpu.VMEM((ROWS, D), BF16),
            pltpu.VMEM((HEADS, HALF, 128), BF16),
            pltpu.VMEM((HEADS, ROWS, 128), BF16),
            pltpu.VMEM((CHIPS, HALF, 128), BF16),
            pltpu.VMEM((CHIPS * 2 * ROWS, 128), BF16),
            pltpu.VMEM((CHIPS * ROWS, 128), BF16),
            pltpu.VMEM((CHIPS * 2 * ROWS, 128), BF16),
            pltpu.VMEM((CHIPS * ROWS, 128), F32),
            pltpu.VMEM((CHIPS * ROWS, 128), F32),
            pltpu.VMEM((CHIPS, HALF, 128), BF16),
            pltpu.VMEM((HEADS, HALF, 128), BF16),
            pltpu.VMEM((ROWS, D), BF16),
            pltpu.VMEM((2, 8, EDGE, 128), F32),
            pltpu.VMEM((2, 8, EDGE, 128), F32),
            pltpu.VMEM((KERNEL, D), F32),
            pltpu.VMEM((1, D), F32),
            dma((9,)), dma((3,)),
            dma((1,)), dma((4,)), dma((1,)), dma((4,)), dma((1,)), dma((4,)), dma((1,)), dma((1,)),
            dma((2,)), dma((2,)),
        ],
        compiler_params=pltpu.CompilerParams(
            collective_id=0, has_side_effects=True, vmem_limit_bytes=GRANT
        ),
        name="block",
    )(
        *(
            pltpu.with_memory_space_constraint(value, pltpu.HBM)
            for value in (
                frames, attend_gain.reshape(1, D), wq, wk, wv, wo, mixer_gain.reshape(1, D), depthwise, bias,
            )
        )
    )
    return pl.pallas_call(
        convolve,
        out_shape=jax.ShapeDtypeStruct((ROWS, D), F32),
        in_specs=[vmem] * 4,
        out_specs=hbm,
        scratch_shapes=[pltpu.VMEM((8, 2, EDGE, 128), F32), dma((2,))],
        compiler_params=pltpu.CompilerParams(vmem_limit_bytes=16 * 1024 * 1024),
        name="convolve",
    )(padded, mixed, depthwise, bias)


def solution(mesh):
    in_specs = (P(("session", "ctx"), None), P(), P(), P(), P(), P(), P(), P(), P())
    return jax.shard_map(
        per_device, mesh=mesh, in_specs=in_specs, out_specs=P(("session", "ctx"), None), check_vma=False
    )
```

```python
import functools
import math

import jax
import jax.numpy as jnp
from jax import lax
from jax.experimental import pallas as pl
from jax.experimental.pallas import tpu as pltpu
from jax.sharding import PartitionSpec as P

F32, BF16 = jnp.float32, jnp.bfloat16
MESH = pl.DeviceIdType.MESH
HEADS = 16
HEAD = 64
KERNEL = 31
ROWS = 192
HALF = ROWS // 2
D = 1024
CHIPS = 16
EDGE = 16
BQ = 4 * ROWS
GRANT = 48 * 1024 * 1024
BK = 8 * ROWS
SCALE = HEAD**-0.5 * math.log2(math.e)
OFFSETS = (
    (0, 0), (0, 1), (0, 7), (1, 0),
    (0, 2), (0, 6), (1, 1), (1, 7),
    (0, 3), (0, 5), (1, 2), (1, 6),
    (0, 4), (1, 3), (1, 5), (1, 4),
)


STEPS = (((0, 0), (1, 0)), ((0, 1), (1, 1)), ((2, 0), (2, 1)), ((3, 0), (3, 1)), ((3, 2), (2, 2)))


def pick(step, table):
    value = jnp.int32(table[0])
    for n in range(1, len(table)):
        if table[n] != table[0]:
            value = jnp.where(step == n, table[n], value)
    return value


def rows_at(index, size):
    if isinstance(index, int):
        return pl.ds(index * size, size)
    return pl.ds(pl.multiple_of(index * size, size), size)


def norm(values, gain):
    center = jnp.mean(values, axis=1, keepdims=True)
    spread = jnp.mean(jnp.square(values - center), axis=1, keepdims=True)
    return (values - center) * lax.rsqrt(spread + 1e-05) * gain


def low_lanes(shape):
    return lax.broadcasted_iota(jnp.int32, shape, 1) < HEAD


def swap(values):
    return pltpu.roll(values, HEAD, 1)


def mix(n, starts, padded, attended, taps_ref, bias_ref, out, shift):
    lanes = rows_at(n, 128)
    taps = taps_ref[:, lanes]
    bias = jnp.broadcast_to(bias_ref[:, lanes], (8, 128))
    for at in starts:
        total = bias
        for tap in range(KERNEL):
            total = total + padded[n, at + tap + 1 : at + tap + 9, :] * taps[tap : tap + 1, :]
        out[n, at - shift : at - shift + 8, :] = attended[n, at : at + 8, :] + total / (1.0 + jnp.exp(-total))


def kernel(
    frames_hbm, again_hbm, wq_hbm, wk_hbm, wv_hbm, wo_hbm, mgain_hbm, taps_hbm, bias_hbm,
    padded, mixed,
    frames, again_ref, wq, wk, wv, wo, mgain_ref, normed,
    sendq, sendkv, qbuf, kvbuf, qx, vx, m_ref, o_ref, sendc, cbuf, context, edges, halos, taps_ref, bias_ref,
    load_sem, own_sem, q_send, q_recv, kv_send, kv_recv, f_send, f_recv, c_send, c_recv, h_send, h_recv,
):
    ctx = lax.axis_index("ctx")
    core = lax.rem(ctx, 2)
    chip = ctx // 2
    z, xh = lax.rem(chip, 8), chip // 8
    partner = chip * 2 + 1 - core

    def toward(r):
        dx, dz = OFFSETS[r]
        return lax.rem(xh + dx, 2) * 8 + lax.rem(z + dz, 8)

    def behind(r):
        dx, dz = OFFSETS[r]
        return lax.rem(xh + dx, 2) * 8 + lax.rem(z + 8 - dz, 8)

    def remote(src, dst, send, recv, target):
        return pltpu.make_async_remote_copy(
            src_ref=src, dst_ref=dst, send_sem=send, recv_sem=recv, device_id={"ctx": target}, device_id_type=MESH
        )
    loads = [
        pltpu.make_async_copy(src, dst, load_sem.at[n])
        for n, (src, dst) in enumerate(
            (
                (frames_hbm, frames), (again_hbm, again_ref),
                (wq_hbm, wq), (wk_hbm, wk), (wv_hbm, wv),
                (wo_hbm, wo), (mgain_hbm, mgain_ref), (taps_hbm, taps_ref), (bias_hbm, bias_ref),
            )
        )
    ]
    for load in loads[:3]:
        load.start()

    barrier = pltpu.get_barrier_semaphore()
    greeted = [toward(r) * 2 + core for r in range(1, CHIPS)]
    greeted += [partner, lax.rem(ctx + 31 + 2 * core, 32)]
    for device in greeted:
        pl.semaphore_signal(barrier, inc=1, device_id={"ctx": device}, device_id_type=MESH)

    loads[0].wait()
    loads[1].wait()
    for load in loads[3:5]:
        load.start()
    normed[...] = norm(frames[...], again_ref[...]).astype(BF16)
    low = low_lanes((ROWS, 128))
    low_half = low_lanes((HALF, 128))
    loads[2].wait()
    for g in range(4):
        q = jnp.dot(normed[...], wq[:, g * 256 : g * 256 + 256], preferred_element_type=F32)
        for pair in range(2):
            piece = q[:, pair * 128 : pair * 128 + 128]
            top, bottom = piece[:HALF], piece[HALF:]
            sendq[4 * g + 2 * pair] = jnp.where(low_half, top, swap(bottom)).astype(BF16)
            sendq[4 * g + 2 * pair + 1] = jnp.where(low_half, swap(top), bottom).astype(BF16)

    def q_copy(r):
        p = toward(r)
        return remote(sendq.at[p], qbuf.at[r], q_send.at[0], q_recv.at[r // 4], p * 2 + core)

    def kv_rows(slot, which):
        return pl.ds(pl.multiple_of((slot * 2 + which) * ROWS, ROWS), ROWS)

    def kv_copy(r):
        p = toward(r)
        return remote(sendkv.at[p], kvbuf.at[kv_rows(r, core)], kv_send.at[0], kv_recv.at[r // 4 if r < 12 else r - 9], p * 2 + core)

    def send(order):
        for kind, r in order:
            (q_copy(r) if kind == "q" else kv_copy(r)).start()

    own_q = pltpu.make_async_copy(sendq.at[chip], qbuf.at[0], own_sem.at[0])
    own_q.start()
    pl.semaphore_wait(barrier, len(greeted))
    send([("q", r) for r in range(1, 8)])
    for load in loads[5:]:
        load.start()
    loads[3].wait()
    loads[4].wait()
    for g in range(4):
        k = jnp.dot(normed[...], wk[:, g * 256 : g * 256 + 256], preferred_element_type=F32)
        v = jnp.dot(normed[...], wv[:, g * 256 : g * 256 + 256], preferred_element_type=F32)
        for pair in range(2):
            kp, vp = k[:, pair * 128 : pair * 128 + 128], v[:, pair * 128 : pair * 128 + 128]
            sendkv[4 * g + 2 * pair] = jnp.where(low, kp, swap(vp)).astype(BF16)
            sendkv[4 * g + 2 * pair + 1] = jnp.where(low, swap(kp), vp).astype(BF16)
    own_kv = pltpu.make_async_copy(sendkv.at[chip], kvbuf.at[kv_rows(0, core)], own_sem.at[1])
    own_forward = remote(sendkv.at[chip], kvbuf.at[kv_rows(0, core)], f_send.at[0], f_recv.at[0], partner)
    own_kv.start()
    own_forward.start()
    send([("kv", r) for r in range(1, 8)] + [("q", r) for r in range(8, CHIPS)] + [("kv", r) for r in range(8, CHIPS)])

    def await_q(block):
        first = 1 if block == 0 else 0
        group = qbuf.at[pl.ds(block * 4 + first, 4 - first)]
        remote(group, group, q_send.at[0], q_recv.at[block], partner).wait_recv()

    def await_kv(chunk):
        group = kvbuf.at[pl.ds(chunk * BK, (3 if chunk == 0 else 4) * ROWS)]
        remote(group, group, kv_send.at[0], kv_recv.at[chunk], partner).wait_recv()

    def forward(slot):
        mine = kvbuf.at[kv_rows(slot, core)]
        return remote(mine, mine, f_send.at[0], f_recv.at[slot // 4], partner)

    def await_forwarded(chunk):
        group = kvbuf.at[pl.ds(chunk * BK, 4 * ROWS)]
        remote(group, group, f_send.at[0], f_recv.at[chunk], partner).wait_recv()

    def reset(n, carry):
        m_ref[rows_at(n, BQ), :] = jnp.full((BQ, 128), -jnp.inf, F32)
        o_ref[rows_at(n, BQ), :] = jnp.zeros((BQ, 128), F32)
        return carry

    lax.fori_loop(0, CHIPS * ROWS // BQ, reset, 0)
    own_q.wait()
    own_kv.wait()
    await_kv(0)
    for r in range(1, 4):
        forward(r).start()

    def unpack_q(block):
        await_q(block)
        for s in range(4):
            x = qbuf[block * 4 + s].astype(F32)
            at = pl.multiple_of((block * 4 + s) * ROWS, ROWS)
            qx[pl.ds(at, HALF), :] = jnp.where(low_half, x, 0.0).astype(BF16)
            qx[pl.ds(at + HALF, HALF), :] = jnp.where(low_half, swap(x), 0.0).astype(BF16)

    def pass_on(chunk):
        if chunk < 3:
            await_kv(chunk)
        for s in range(4):
            if chunk == 3:
                piece = kvbuf.at[kv_rows(12 + s, core)]
                remote(piece, piece, kv_send.at[0], kv_recv.at[3 + s], partner).wait_recv()
            forward(chunk * 4 + s).start()

    low_wide = low_lanes((8 * ROWS, 128))

    def open_chunk(chunk):
        await_forwarded(chunk)
        at = rows_at(chunk, BK)
        x = kvbuf[at, :]
        vx[at, :] = jnp.where(low_wide, jnp.ones_like(x), x)

    def attend(i, j, size=BQ):
        rows = rows_at(i, size)
        q = qx[rows, :]
        scores = lax.dot_general(
            q, kvbuf[rows_at(j, BK), :], (((1,), (1,)), ((), ())), preferred_element_type=F32
        )
        old = m_ref[rows, :]
        new = jnp.maximum(old, jnp.max(scores, axis=1, keepdims=True))
        weights = jnp.exp2((scores - jnp.concatenate([new] * (BK // 128), axis=1)) * SCALE).astype(BF16)
        part = jnp.dot(weights, vx[rows_at(j, BK), :], preferred_element_type=F32)
        o_ref[rows, :] = o_ref[rows, :] * jnp.exp2((old - new) * SCALE) + part
        m_ref[rows, :] = new

    def give_back(slots):
        for r in slots:
            o = o_ref[r * ROWS : (r + 1) * ROWS, :]
            c = o / swap(o)
            sendc[r] = jnp.where(low_half, swap(c[:HALF]), c[HALF:]).astype(BF16)
        for r in slots:
            if r > 0:
                remote(sendc.at[r], cbuf.at[chip], c_send.at[0], c_recv.at[0], behind(r) * 2 + core).start()
    unpack_q(0)
    unpack_q(1)

    def step(t, carry):
        opened = {0: 0, 1: 1, 4: 2}
        for when, chunk in opened.items():
            @pl.when(t == when)
            def _():
                open_chunk(chunk)
        for when, block in {2: 2, 3: 3}.items():
            @pl.when(t == when)
            def _():
                unpack_q(block)
        for half in range(2):
            attend(pick(t, [pair[half][0] for pair in STEPS]), pick(t, [pair[half][1] for pair in STEPS]))
        for when, chunk in {0: 1, 3: 2, 4: 3}.items():
            @pl.when(t == when)
            def _():
                pass_on(chunk)

        return carry
    lax.fori_loop(0, len(STEPS), step, 0)
    attend(1, 2)
    open_chunk(3)
    for half in (6, 7):
        attend(half, 3, 2 * ROWS)
        give_back(range(2 * half, 2 * half + 2))
    attend(2, 3)
    attend(1, 3)
    give_back(range(8, 12))
    give_back(range(4, 8))
    attend(0, 2)
    attend(0, 3)
    give_back(range(4))

    own_c = pltpu.make_async_copy(sendc.at[0], cbuf.at[chip], own_sem.at[2])
    own_c.start()
    for load in loads[5:]:
        load.wait()
    own_c.wait()
    returned = cbuf.at[pl.ds(0, CHIPS - 1)]
    remote(returned, returned, c_send.at[0], c_recv.at[0], partner).wait_recv()
    for pair in range(HEADS // 2):
        a, b = cbuf[2 * pair].astype(F32), cbuf[2 * pair + 1].astype(F32)
        cols = slice(pair * 128, pair * 128 + 128)
        context[:HALF, cols] = jnp.where(low_half, a, swap(b)).astype(BF16)
        context[HALF:, cols] = jnp.where(low_half, swap(a), b).astype(BF16)
    total = frames[...] + jnp.dot(context[...], wo[...], preferred_element_type=F32)
    mixer_in = norm(total, mgain_ref[...])
    for n in range(8):
        part = mixer_in[:, n * 128 : n * 128 + 128]
        edges[0, n] = part[:EDGE]
        edges[1, n] = part[ROWS - EDGE :]
        padded[n, EDGE : EDGE + ROWS, :] = part
        mixed[n] = total[:, n * 128 : n * 128 + 128]

    after, before = lax.rem(ctx + 1, 32), lax.rem(ctx + 31, 32)
    up = remote(edges.at[1], halos.at[0], h_send.at[0], h_recv.at[0], after)
    down = remote(edges.at[0], halos.at[1], h_send.at[1], h_recv.at[1], before)
    up.start()
    down.start()

    def interior(n, carry):
        mix(n, range(EDGE, ROWS - EDGE, 8), padded, mixed, taps_ref, bias_ref, mixed, 0)
        return carry

    lax.fori_loop(0, 8, interior, 0)
    up.wait()
    down.wait()
    padded[:, :EDGE, :] = jnp.where(ctx > 0, halos[0], 0.0)
    padded[:, EDGE + ROWS :, :] = jnp.where(ctx < 31, halos[1], 0.0)
    remote(qbuf.at[pl.ds(0, CHIPS - 1)], qbuf.at[pl.ds(0, CHIPS - 1)], q_send.at[0], q_recv.at[0], partner).wait_send()
    for sem, slots in ((kv_send, CHIPS - 1), (f_send, CHIPS)):
        group = kvbuf.at[pl.ds(0, slots * ROWS)]
        remote(group, group, sem.at[0], kv_recv.at[0], partner).wait_send()
    remote(returned, returned, c_send.at[0], c_recv.at[0], partner).wait_send()


def convolve(padded_ref, mixed_ref, taps_ref, bias_ref, out_hbm, result, sems):
    def inner(n):
        rows = pl.ds(EDGE, ROWS - 2 * EDGE)
        return pltpu.make_async_copy(mixed_ref.at[n, rows], out_hbm.at[rows, rows_at(n, 128)], sems.at[0])

    def edge(n, side):
        rows = pl.ds(side * (ROWS - EDGE), EDGE)
        return pltpu.make_async_copy(result.at[n, side], out_hbm.at[rows, rows_at(n, 128)], sems.at[1])

    for n in range(8):
        inner(n).start()

    def column(n, carry):
        mix(n, range(0, EDGE, 8), padded_ref, mixed_ref, taps_ref, bias_ref, result.at[:, 0], 0)
        mix(n, range(ROWS - EDGE, ROWS, 8), padded_ref, mixed_ref, taps_ref, bias_ref, result.at[:, 1], ROWS - EDGE)
        edge(n, 0).start()
        edge(n, 1).start()
        return carry

    lax.fori_loop(0, 8, column, 0)
    block = mixed_ref.at[:, pl.ds(EDGE, ROWS - 2 * EDGE)]
    pltpu.make_async_copy(block, block, sems.at[0]).wait()
    pltpu.make_async_copy(result, result, sems.at[1]).wait()


def per_device(frames, attend_gain, wq, wk, wv, wo, mixer_gain, depthwise, mixer_bias):
    hbm = pl.BlockSpec(memory_space=pltpu.HBM)
    vmem = pl.BlockSpec(memory_space=pltpu.VMEM)
    dma = pltpu.SemaphoreType.DMA
    bias = mixer_bias.reshape(1, D)
    padded, mixed = pl.pallas_call(
        kernel,
        out_shape=(
            jax.ShapeDtypeStruct((8, ROWS + 2 * EDGE, 128), F32),
            jax.ShapeDtypeStruct((8, ROWS, 128), F32),
        ),
        in_specs=[hbm] * 9,
        out_specs=(vmem, vmem),
        scratch_shapes=[
            pltpu.VMEM((ROWS, D), F32),
            pltpu.VMEM((1, D), F32),
            *[pltpu.VMEM((D, D), BF16)] * 4,
            pltpu.VMEM((1, D), F32),
            pltpu.VMEM((ROWS, D), BF16),
            pltpu.VMEM((HEADS, HALF, 128), BF16),
            pltpu.VMEM((HEADS, ROWS, 128), BF16),
            pltpu.VMEM((CHIPS, HALF, 128), BF16),
            pltpu.VMEM((CHIPS * 2 * ROWS, 128), BF16),
            pltpu.VMEM((CHIPS * ROWS, 128), BF16),
            pltpu.VMEM((CHIPS * 2 * ROWS, 128), BF16),
            pltpu.VMEM((CHIPS * ROWS, 128), F32),
            pltpu.VMEM((CHIPS * ROWS, 128), F32),
            pltpu.VMEM((CHIPS, HALF, 128), BF16),
            pltpu.VMEM((HEADS, HALF, 128), BF16),
            pltpu.VMEM((ROWS, D), BF16),
            pltpu.VMEM((2, 8, EDGE, 128), F32),
            pltpu.VMEM((2, 8, EDGE, 128), F32),
            pltpu.VMEM((KERNEL, D), F32),
            pltpu.VMEM((1, D), F32),
            dma((9,)), dma((3,)),
            dma((1,)), dma((4,)), dma((1,)), dma((7,)), dma((1,)), dma((4,)), dma((1,)), dma((1,)),
            dma((2,)), dma((2,)),
        ],
        compiler_params=pltpu.CompilerParams(
            collective_id=0, has_side_effects=True, vmem_limit_bytes=GRANT
        ),
        name="block",
    )(
        *(
            pltpu.with_memory_space_constraint(value, pltpu.HBM)
            for value in (
                frames, attend_gain.reshape(1, D), wq, wk, wv, wo, mixer_gain.reshape(1, D), depthwise, bias,
            )
        )
    )
    return pl.pallas_call(
        convolve,
        out_shape=jax.ShapeDtypeStruct((ROWS, D), F32),
        in_specs=[vmem] * 4,
        out_specs=hbm,
        scratch_shapes=[pltpu.VMEM((8, 2, EDGE, 128), F32), dma((2,))],
        compiler_params=pltpu.CompilerParams(vmem_limit_bytes=16 * 1024 * 1024),
        name="convolve",
    )(padded, mixed, depthwise, bias)


def solution(mesh):
    in_specs = (P(("session", "ctx"), None), P(), P(), P(), P(), P(), P(), P(), P())
    return jax.shard_map(
        per_device, mesh=mesh, in_specs=in_specs, out_specs=P(("session", "ctx"), None), check_vma=False
    )
```
